32 devices in a mesh: gx: 2 (over x), gy: 4 (over z), gz: 4 (over y, core).
Axes of the slice: x: 2, y: 2, z: 4, core: 2. Of those that a mesh axis runs over, the one named last changes fastest.
Arguments:
- inputs: bfloat16 [512, 6144], P(('gx', 'gz'), 'gy'), may hold values from -6 to 6
- norm_gain: float32 [6144], P('gy'), may hold values from 0.25 to 1.75
- norm_bias: float32 [6144], P('gy'), may hold values from -4 to 4
- pre_act: bfloat16 [512, 24576], P(('gx', 'gy'), 'gz'), may hold values from -8 to 8
- grad_act: bfloat16 [512, 24576], P(('gx', 'gy'), 'gz'), may hold values from -4 to 4
- up_weight: bfloat16 [4, 6144, 6144], P('gz', 'gx', 'gy'), may hold values from -0.078125 to 0.078125
Outputs:
- grad_inputs: bfloat16 [512, 6144], P(('gx', 'gz'), 'gy')
- grad_gain: float32 [6144], P('gy')
- grad_bias: float32 [6144], P('gy')
- grad_weight: float32 [4, 6144, 6144], P('gz', 'gx', 'gy')
The draws below stay inside these ranges and needn't reach their ends.
All inputs are finite; a program needn't handle non-finite values.
Results may differ from the reference program's by a relative error of at most 0.0049.
Values may be sent and summed in bfloat16 or wider, within the bound.
A program may use at most 128 MiB of HBM per device.

```python
import jax
import jax.numpy as jnp
from jax import lax

D = 6144
FF = 24576
TOKENS = 512
FB = 6144
N_GZ = 4


def block_levels(stream_key, extent, pieces, low, top_value):
    gain, own = 1.0, jax.random.fold_in(stream_key, 6)
    for dim, parts in pieces:
        heights = jnp.exp(jax.random.uniform(jax.random.fold_in(own, dim), (parts,), jnp.float32, low / len(pieces), top_value / len(pieces)))
        gain = gain * jnp.repeat(heights, extent[dim] // parts).reshape([-1 if axis == dim else 1 for axis in range(len(extent))])
    return gain


def noise(own_key, extent, deviation, bound, shards=(), dtype=jnp.bfloat16):
    array = deviation * jax.random.normal(own_key, extent, jnp.float32)
    if shards:
        array = array * block_levels(own_key, extent, shards, -0.22, 0.18)
    return jnp.clip(array, -bound, bound).astype(dtype)


def setup_inputs(seed: int = 0) -> dict:
    seeds = jax.random.split(jax.random.key(seed), 7)
    return {
        "inputs": noise(seeds[0], (TOKENS, D), 1.0, 6.0, ((0, 8), (1, 4))),
        "norm_gain": jnp.clip(1.0 + 0.15 * jax.random.normal(seeds[1], (D,), jnp.float32), 0.25, 1.75),
        "norm_bias": noise(seeds[2], (D,), 0.7, 4.0, ((0, 4),), jnp.float32),
        "pre_act": noise(seeds[3], (TOKENS, FF), 1.5, 8.0, ((0, 8), (1, 4))),
        "grad_act": noise(seeds[4], (TOKENS, FF), 0.5, 4.0, ((0, 8), (1, 4))),
        "up_weight": noise(seeds[5], (N_GZ, FB, D), D ** -0.5, 0.078125, ((0, 4), (1, 2), (2, 4))),
    }


epsilon = 1e-05
root_half = 0.7071067811865476
gauss_norm = 0.3989422804014327

def reference(inputs, norm_gain, norm_bias, pre_act, grad_act, up_weight):
    widened = inputs.astype(jnp.float32)
    row_mean = lax.optimization_barrier(jnp.mean(widened, axis=1, keepdims=True))
    centred = widened - row_mean
    row_var = lax.optimization_barrier(jnp.mean(centred * centred, axis=1, keepdims=True))
    inv_std = lax.rsqrt(row_var + epsilon)
    x_hat = centred * inv_std
    normed = (x_hat * norm_gain + norm_bias).astype(jnp.bfloat16)
    pre_float = pre_act.astype(jnp.float32)
    slopes = 0.5 * (1.0 + jax.scipy.special.erf(pre_float * root_half)) + pre_float * jnp.exp(-0.5 * pre_float * pre_float) * gauss_norm
    grad_pre = (grad_act.astype(jnp.float32) * slopes).astype(jnp.bfloat16)
    weight = up_weight.reshape(FF, D)
    grad_normed = jnp.dot(grad_pre, weight, preferred_element_type=jnp.float32)
    grad_weight = lax.dot_general(grad_pre, normed, (((0,), (0,)), ((), ())), preferred_element_type=jnp.float32)
    grad_weight = grad_weight.reshape(N_GZ, FF // N_GZ, D)
    grad_gain = lax.optimization_barrier(jnp.sum(grad_normed * x_hat, axis=0))
    grad_bias = lax.optimization_barrier(jnp.sum(grad_normed, axis=0))
    scaled = grad_normed * norm_gain
    grad_inputs = inv_std * (scaled - lax.optimization_barrier(jnp.mean(scaled, axis=1, keepdims=True)) - x_hat * lax.optimization_barrier(jnp.mean(scaled * x_hat, axis=1, keepdims=True)))
    return (grad_inputs.astype(jnp.bfloat16), grad_gain, grad_bias, grad_weight)
```

```python
import jax
import jax.numpy as jnp
from jax import lax
from jax.sharding import PartitionSpec as P

D = 6144


epsilon = 1e-05
root_half = 0.7071067811865476
gauss_norm = 0.3989422804014327


def on_device(inputs, norm_gain, norm_bias, pre_act, grad_act, up_weight):
    widened = inputs.astype(jnp.float32)
    totals = lax.psum(jnp.sum(widened, axis=1), "gy")
    row_mean = totals / D
    centred = widened - row_mean[:, None]
    row_var = lax.psum(jnp.sum(centred * centred, axis=1), "gy") / D
    inv_std = lax.rsqrt(row_var + epsilon)[:, None]
    x_hat = centred * inv_std
    normed = (x_hat * norm_gain + norm_bias).astype(jnp.bfloat16)
    pre_float = pre_act.astype(jnp.float32)
    slopes = (
        0.5 * (1.0 + jax.scipy.special.erf(pre_float * root_half))
        + pre_float * jnp.exp(-0.5 * pre_float * pre_float) * gauss_norm
    )
    grad_local = (grad_act.astype(jnp.float32) * slopes).astype(jnp.bfloat16)
    grad_rows = lax.all_gather(grad_local, "gy", axis=0, tiled=True)
    grad_cols = lax.all_to_all(grad_rows, "gx", split_axis=1, concat_axis=0, tiled=True)
    partial_value = jnp.dot(grad_cols, up_weight[0], preferred_element_type=jnp.float32)
    grad_normed = lax.psum_scatter(
        partial_value, ("gx", "gz"), scatter_dimension=0, tiled=True
    )
    normed_all = lax.all_gather(normed, ("gx", "gz"), axis=0, tiled=True)
    weight_block = lax.dot_general(
        grad_cols, normed_all, (((0,), (0,)), ((), ())), preferred_element_type=jnp.float32
    )
    grad_weight = weight_block.reshape(up_weight.shape)
    grad_gain, grad_bias = lax.psum(
        (jnp.sum(grad_normed * x_hat, axis=0), jnp.sum(grad_normed, axis=0)), ("gx", "gz")
    )
    scaled = grad_normed * norm_gain
    grad_sum, grad_dot = lax.psum((jnp.sum(scaled, axis=1), jnp.sum(scaled * x_hat, axis=1)), "gy")
    grad_inputs = inv_std * (scaled - grad_sum[:, None] / D - x_hat * (grad_dot[:, None] / D))
    return (grad_inputs.astype(jnp.bfloat16), grad_gain, grad_bias, grad_weight)


def solution(mesh):
    in_specs = (
        P(("gx", "gz"), "gy"),
        P("gy"),
        P("gy"),
        P(("gx", "gy"), "gz"),
        P(("gx", "gy"), "gz"),
        P("gz", "gx", "gy"),
    )
    out_specs = (P(("gx", "gz"), "gy"), P("gy"), P("gy"), P("gz", "gx", "gy"))
    return jax.shard_map(
        on_device, mesh=mesh, in_specs=in_specs, out_specs=out_specs, check_vma=False
    )
```

```python
import functools

import jax
import jax.numpy as jnp
from jax import lax
from jax.experimental import pallas as pl
from jax.experimental.pallas import tpu as pltpu
from jax.sharding import PartitionSpec as P

MESH = pl.DeviceIdType.MESH
LANES = 128
SUB = 8
CHUNK = 256

epsilon = 1e-05
root_half = 0.7071067811865476
gauss_norm = 0.3989422804014327


def to_tile(pad, first, second, rows):
    lane = lax.broadcasted_iota(jnp.int32, (rows, LANES), 1)
    pad[...] = jnp.zeros_like(pad)
    pad[:rows, :] = jnp.where(lane == 0, first, jnp.where(lane == 1, second, 0.0))
    return pad[...].T[:SUB, :]


def to_columns(pad, tile, rows):
    pad[...] = jnp.zeros_like(pad)
    pad[:SUB, :] = tile
    flipped = pad[...].T
    return flipped[:rows, 0:1], flipped[:rows, 1:2]


def kernel(
    sizes,
    inputs, gain, bias, grad_local, weight,
    cols_out, normed_out, grad_inputs, grad_sums,
    w_buf, cols, part_send, part_recv, x_hat, grad_normed, normed_own, sums, pad, stat_a, stat_b,
    w_sem, own_sem, out_sem, z_recv, right_send, left_send, x_send,
    stat_send, stat_recv, norm_send, norm_recv, norm_own_sem, part_ssem, part_rsem, part_own_sem,
    sums_send, sums_recv, last_send, last_recv,
):
    n_gx, n_gy, n_gz, rows, rows_in, width, depth = sizes
    ratio = rows // rows_in
    plane = n_gx * n_gz
    g, p, t = lax.axis_index("gx"), lax.axis_index("gy"), lax.axis_index("gz")
    me = g * n_gz + t
    model = width * n_gy

    def line_peer(i):
        return lax.rem(p + i, n_gy)

    def plane_peer(i):
        other = lax.rem(me + i, plane)
        return other, {"gx": other // n_gz, "gz": lax.rem(other, n_gz)}

    def slot(q, u):
        return q * n_gx + u

    barrier = pltpu.get_barrier_semaphore()
    for i in range(1, n_gy):
        pl.semaphore_signal(barrier, inc=1, device_id={"gy": line_peer(i)}, device_id_type=MESH)

    @pl.loop(1, plane)
    def _(i):
        pl.semaphore_signal(barrier, inc=1, device_id=plane_peer(i)[1], device_id_type=MESH)

    own = pltpu.make_async_copy(
        grad_local.at[:, pl.ds(pl.multiple_of(g * depth, LANES), depth)], cols.at[p, g], own_sem
    )
    own.start()
    w_copy = pltpu.make_async_copy(weight, w_buf, w_sem)
    w_copy.start()

    widened = inputs[...].astype(jnp.float32)
    mean_here = jnp.sum(widened, axis=1, keepdims=True) / width
    centred = widened - mean_here
    square_here = jnp.sum(centred * centred, axis=1, keepdims=True)
    stat_a[p] = to_tile(pad, mean_here, square_here, rows_in)

    pl.semaphore_wait(barrier, n_gy - 1 + plane - 1)

    def tile_copy(buf, i, ssem, rsem, source):
        return pltpu.make_async_remote_copy(
            src_ref=buf.at[source], dst_ref=buf.at[source],
            send_sem=ssem.at[line_peer(i)], recv_sem=rsem.at[source],
            device_id={"gy": line_peer(i)}, device_id_type=MESH,
        )

    for i in range(1, n_gy):
        tile_copy(stat_a, i, stat_send, stat_recv, p).start()

    def x_copy(i, source):
        u = lax.rem(g + i, n_gx)
        return pltpu.make_async_remote_copy(
            src_ref=grad_local.at[:, pl.ds(pl.multiple_of(u * depth, LANES), depth)],
            dst_ref=cols.at[p, source],
            send_sem=x_send.at[u], recv_sem=z_recv.at[slot(p, source)],
            device_id={"gx": u}, device_id_type=MESH,
        )

    def z_copy(q, u, step, sems):
        return pltpu.make_async_remote_copy(
            src_ref=cols.at[q, u], dst_ref=cols.at[q, u],
            send_sem=sems.at[slot(q, u)], recv_sem=z_recv.at[slot(q, u)],
            device_id={"gy": lax.rem(p + step + n_gy, n_gy)}, device_id_type=MESH,
        )

    def out_copy(q, u):
        return pltpu.make_async_copy(cols.at[q, u], cols_out.at[u, q], out_sem.at[slot(q, u)])

    def pass_right(q, u):
        @pl.when(p + 1 < n_gy)
        def _():
            z_copy(q, u, 1, right_send).start()

    def pass_left(q, u):
        @pl.when(p >= 1)
        def _():
            z_copy(q, u, -1, left_send).start()

    for i in range(1, n_gx):
        x_copy(i, g).start()
    own.wait()
    pass_right(p, g)
    pass_left(p, g)
    out_copy(p, g).start()

    for i in range(1, n_gy):
        tile_copy(stat_a, i, stat_send, stat_recv, line_peer(i)).wait_recv()
    columns = [to_columns(pad, stat_a[q], rows_in) for q in range(n_gy)]
    mean = sum(c[0] for c in columns) / n_gy
    total = sum(c[1] + width * (c[0] - mean) * (c[0] - mean) for c in columns)
    inv_std = lax.rsqrt(total / model + epsilon)
    x_hat[...] = (inputs[...].astype(jnp.float32) - mean) * inv_std
    normed_own[...] = (x_hat[...] * gain[...] + bias[...]).astype(jnp.bfloat16)

    def norm_copy(i, source):
        other, where = plane_peer(i)
        return pltpu.make_async_remote_copy(
            src_ref=normed_own, dst_ref=normed_out.at[source],
            send_sem=norm_send.at[other], recv_sem=norm_recv.at[source],
            device_id=where, device_id_type=MESH,
        )

    @pl.loop(1, plane)
    def _(i):
        norm_copy(i, me).start()

    norm_own = pltpu.make_async_copy(normed_own, normed_out.at[me], norm_own_sem)
    norm_own.start()

    for i in range(1, n_gx):
        u = lax.rem(g + i, n_gx)
        x_copy(i, u).wait_recv()
        pass_right(p, u)
        pass_left(p, u)
        out_copy(p, u).start()
    w_copy.wait()

    def part_copy(q, u, j, source):
        owner = q * ratio + j
        return pltpu.make_async_remote_copy(
            src_ref=part_send.at[q, u, j], dst_ref=part_recv.at[source],
            send_sem=part_ssem.at[u * n_gz + owner], recv_sem=part_rsem.at[source],
            device_id={"gx": u, "gz": owner}, device_id_type=MESH,
        )

    def part_keep(q, u, j):
        return pltpu.make_async_copy(part_send.at[q, u, j], part_recv.at[me], part_own_sem)

    def multiply(q):
        @pl.loop(0, width // CHUNK)
        def _(c):
            span = pl.ds(pl.multiple_of(c * CHUNK, CHUNK), CHUNK)
            block = cols[q].reshape(n_gx * rows, depth)
            value = jnp.dot(block, w_buf[:, span], preferred_element_type=jnp.float32)
            part_send[q, :, :, :, span] = value.astype(jnp.bfloat16).reshape(
                n_gx, ratio, rows_in, CHUNK
            )

        for u in range(n_gx):
            for j in range(ratio):
                mine = jnp.logical_and(u == g, q * ratio + j == t)

                @pl.when(mine)
                def _():
                    part_keep(q, u, j).start()

                @pl.when(jnp.logical_not(mine))
                def _():
                    part_copy(q, u, j, me).start()

    multiply(p)

    @pl.loop(1, n_gy)
    def _(s):
        for k in range(n_gx):
            u = lax.rem(g + k, n_gx)

            @pl.when(p - s >= 0)
            def _():
                z_copy(p - s, u, 1, right_send).wait_recv()
                pass_right(p - s, u)
                out_copy(p - s, u).start()

            @pl.when(p + s < n_gy)
            def _():
                z_copy(p + s, u, -1, left_send).wait_recv()
                pass_left(p + s, u)
                out_copy(p + s, u).start()

        @pl.loop(0, 2)
        def _(side):
            q = p + (2 * side - 1) * s

            @pl.when(jnp.logical_and(q >= 0, q < n_gy))
            def _():
                multiply(q)

    part_keep(0, 0, 0).wait()

    @pl.loop(1, plane)
    def _(i):
        other, where = plane_peer(i)
        pltpu.make_async_remote_copy(
            src_ref=part_send.at[0, 0, 0], dst_ref=part_recv.at[other],
            send_sem=part_ssem.at[other], recv_sem=part_rsem.at[other],
            device_id=where, device_id_type=MESH,
        ).wait_recv()

    row_sum = jnp.zeros((rows_in, 1), jnp.float32)
    row_dot = jnp.zeros((rows_in, 1), jnp.float32)
    for start in range(0, width, CHUNK):
        span = slice(start, start + CHUNK)
        block = lax.fori_loop(
            0, plane,
            lambda i, acc: acc + part_recv[i, :, span].astype(jnp.float32),
            jnp.zeros((rows_in, CHUNK), jnp.float32),
        )
        grad_normed[:, span] = block
        hat = x_hat[:, span]
        sums[me, 0:1, span] = jnp.sum(block * hat, axis=0, keepdims=True)
        sums[me, 1:2, span] = jnp.sum(block, axis=0, keepdims=True)
        scaled = block * gain[:, span]
        row_sum = row_sum + jnp.sum(scaled, axis=1, keepdims=True)
        row_dot = row_dot + jnp.sum(scaled * hat, axis=1, keepdims=True)
    stat_b[p] = to_tile(pad, row_sum, row_dot, rows_in)
    for i in range(1, n_gy):
        tile_copy(stat_b, i, last_send, last_recv, p).start()

    def sums_copy(i, source):
        other, where = plane_peer(i)
        return pltpu.make_async_remote_copy(
            src_ref=sums.at[source], dst_ref=sums.at[source],
            send_sem=sums_send.at[other], recv_sem=sums_recv.at[source],
            device_id=where, device_id_type=MESH,
        )

    @pl.loop(1, plane)
    def _(i):
        sums_copy(i, me).start()

    for i in range(1, n_gy):
        tile_copy(stat_b, i, last_send, last_recv, line_peer(i)).wait_recv()
    both = stat_b[0]
    for q in range(1, n_gy):
        both = both + stat_b[q]
    grad_sum, grad_dot = to_columns(pad, both, rows_in)
    for start in range(0, width, CHUNK):
        span = slice(start, start + CHUNK)
        scaled = grad_normed[:, span] * gain[:, span]
        grad_inputs[:, span] = (
            inv_std * (scaled - grad_sum / model - x_hat[:, span] * (grad_dot / model))
        ).astype(jnp.bfloat16)

    @pl.loop(1, plane)
    def _(i):
        sums_copy(i, plane_peer(i)[0]).wait_recv()

    grad_sums[...] = lax.fori_loop(
        0, plane, lambda i, acc: acc + sums[i], jnp.zeros((2, width), jnp.float32)
    )

    norm_own.wait()

    @pl.loop(1, plane)
    def _(i):
        other, where = plane_peer(i)
        norm_copy(i, me).wait_send()
        norm_copy(i, other).wait_recv()
        sums_copy(i, me).wait_send()
        pltpu.make_async_remote_copy(
            src_ref=part_send.at[0, 0, 0], dst_ref=part_recv.at[me],
            send_sem=part_ssem.at[other], recv_sem=part_rsem.at[me],
            device_id=where, device_id_type=MESH,
        ).wait_send()

    for i in range(1, n_gy):
        tile_copy(stat_a, i, stat_send, stat_recv, p).wait_send()
        tile_copy(stat_b, i, last_send, last_recv, p).wait_send()
    for i in range(1, n_gx):
        x_copy(i, g).wait_send()

    @pl.loop(0, n_gy)
    def _(q):
        for u in range(n_gx):
            out_copy(q, u).wait()

            @pl.when(jnp.logical_and(q <= p, p + 1 < n_gy))
            def _():
                z_copy(q, u, 1, right_send).wait_send()

            @pl.when(jnp.logical_and(q >= p, p >= 1))
            def _():
                z_copy(q, u, -1, left_send).wait_send()


def on_device(shape, inputs, norm_gain, norm_bias, pre_act, grad_act, up_weight):
    n_gx, n_gy, n_gz = shape["gx"], shape["gy"], shape["gz"]
    plane = n_gx * n_gz
    rows_in, width = inputs.shape
    rows = pre_act.shape[0]
    depth = up_weight.shape[1]
    ratio = rows // rows_in
    pre_float = pre_act.astype(jnp.float32)
    slopes = (
        0.5 * (1.0 + jax.scipy.special.erf(pre_float * root_half))
        + pre_float * jnp.exp(-0.5 * pre_float * pre_float) * gauss_norm
    )
    grad_local = (grad_act.astype(jnp.float32) * slopes).astype(jnp.bfloat16)
    whole, vmem = pl.BlockSpec(memory_space=pl.ANY), pl.BlockSpec(memory_space=pltpu.VMEM)
    dma = pltpu.SemaphoreType.DMA
    bf16, f32 = jnp.bfloat16, jnp.float32
    slots = n_gx * n_gy
    grad_cols, normed_all, grad_inputs, grad_sums = pl.pallas_call(
        functools.partial(kernel, (n_gx, n_gy, n_gz, rows, rows_in, width, depth)),
        out_shape=(
            jax.ShapeDtypeStruct((n_gx, n_gy, rows, depth), bf16),
            jax.ShapeDtypeStruct((plane, rows_in, width), bf16),
            jax.ShapeDtypeStruct((rows_in, width), bf16),
            jax.ShapeDtypeStruct((2, width), f32),
        ),
        in_specs=[vmem, vmem, vmem, whole, whole],
        out_specs=(whole, whole, vmem, vmem),
        scratch_shapes=[
            pltpu.VMEM((depth, width), bf16),
            pltpu.VMEM((n_gy, n_gx, rows, depth), bf16),
            pltpu.VMEM((n_gy, n_gx, ratio, rows_in, width), bf16),
            pltpu.VMEM((plane, rows_in, width), bf16),
            pltpu.VMEM((rows_in, width), f32),
            pltpu.VMEM((rows_in, width), f32),
            pltpu.VMEM((rows_in, width), bf16),
            pltpu.VMEM((plane, 2, width), f32),
            pltpu.VMEM((LANES, LANES), f32),
            pltpu.VMEM((n_gy, SUB, LANES), f32),
            pltpu.VMEM((n_gy, SUB, LANES), f32),
            dma, dma, dma((slots,)), dma((slots,)), dma((slots,)), dma((slots,)), dma((n_gx,)),
            dma((n_gy,)), dma((n_gy,)), dma((plane,)), dma((plane,)), dma,
            dma((plane,)), dma((plane,)), dma,
            dma((plane,)), dma((plane,)), dma((n_gy,)), dma((n_gy,)),
        ],
        compiler_params=pltpu.CompilerParams(
            collective_id=0, has_side_effects=True, vmem_limit_bytes=60 * 1024 * 1024
        ),
    )(inputs, norm_gain[None], norm_bias[None], grad_local, up_weight[0])
    tokens = slots * rows
    weight_block = lax.dot_general(
        grad_cols.reshape(tokens, depth),
        normed_all.reshape(tokens, width),
        (((0,), (0,)), ((), ())),
        preferred_element_type=jnp.float32,
    )
    return grad_inputs, grad_sums[0], grad_sums[1], weight_block.reshape(up_weight.shape)


def solution(mesh):
    in_specs = (
        P(("gx", "gz"), "gy"),
        P("gy"),
        P("gy"),
        P(("gx", "gy"), "gz"),
        P(("gx", "gy"), "gz"),
        P("gz", "gx", "gy"),
    )
    out_specs = (P(("gx", "gz"), "gy"), P("gy"), P("gy"), P("gz", "gx", "gy"))
    return jax.shard_map(
        functools.partial(on_device, dict(mesh.shape)),
        mesh=mesh, in_specs=in_specs, out_specs=out_specs, check_vma=False,
    )
```

```python
import functools

import jax
import jax.numpy as jnp
from jax import lax
from jax.experimental import pallas as pl
from jax.experimental.pallas import tpu as pltpu
from jax.sharding import PartitionSpec as P

MESH = pl.DeviceIdType.MESH
LANES = 128
SUB = 8
CHUNK = 256
SEND = 512

epsilon = 1e-05
root_half = 0.7071067811865476
gauss_norm = 0.3989422804014327


def to_tile(pad, first, second, rows):
    lane = lax.broadcasted_iota(jnp.int32, (rows, LANES), 1)
    pad[...] = jnp.zeros_like(pad)
    pad[:rows, :] = jnp.where(lane == 0, first, jnp.where(lane == 1, second, 0.0))
    return pad[...].T[:SUB, :]


def to_columns(pad, tile, rows):
    pad[...] = jnp.zeros_like(pad)
    pad[:SUB, :] = tile
    flipped = pad[...].T
    return flipped[:rows, 0:1], flipped[:rows, 1:2]


def kernel(
    sizes,
    inputs, gain, bias, pre_act, grad_act, weight,
    cols_out, normed_out, grad_inputs, grad_gain, grad_bias,
    pre_buf, act_buf, stage, w_buf, cols, part_send, part_recv, x_hat, grad_normed, normed_own, sums, pad, stat_a, stat_b,
    pre_sem, act_sem, w_sem, out_sem, z_recv, right_send, left_send, x_send,
    stat_send, stat_recv, norm_send, norm_recv, norm_own_sem, part_ssem, part_rsem, part_own_sem,
    sums_send, sums_recv, last_send, last_recv,
):
    n_gx, n_gy, n_gz, rows, rows_in, width, depth = sizes
    ratio = rows // rows_in
    plane = n_gx * n_gz
    g, p, t = lax.axis_index("gx"), lax.axis_index("gy"), lax.axis_index("gz")
    me = g * n_gz + t
    model = width * n_gy

    def line_peer(i):
        return lax.rem(p + i, n_gy)

    def plane_peer(i):
        other = lax.rem(me + i, plane)
        return other, {"gx": other // n_gz, "gz": lax.rem(other, n_gz)}

    def slot(q, u):
        return q * n_gx + u

    def row(ref, span):
        return ref[span].reshape(1, -1)

    barrier = pltpu.get_barrier_semaphore()
    for i in range(1, n_gy):
        pl.semaphore_signal(barrier, inc=1, device_id={"gy": line_peer(i)}, device_id_type=MESH)

    @pl.loop(1, plane)
    def _(i):
        pl.semaphore_signal(barrier, inc=1, device_id=plane_peer(i)[1], device_id_type=MESH)

    def half(ref, u):
        return ref.at[:, pl.ds(pl.multiple_of(u * depth, LANES), depth)]

    loads = []
    for i in list(range(1, n_gx)) + [0]:
        u = lax.rem(g + i, n_gx)
        pair = (
            pltpu.make_async_copy(half(pre_act, u), pre_buf.at[u], pre_sem.at[u]),
            pltpu.make_async_copy(half(grad_act, u), act_buf.at[u], act_sem.at[u]),
        )
        for copy in pair:
            copy.start()
        loads.append((u, pair))
    w_copy = pltpu.make_async_copy(weight, w_buf, w_sem)
    w_copy.start()

    step = next(n for n in (384, 256, LANES) if depth % n == 0)

    def gelu_grad(u, pair, out):
        for copy in pair:
            copy.wait()

        @pl.loop(0, depth // step)
        def _(c):
            span = pl.ds(pl.multiple_of(c * step, step), step)
            pre = pre_buf[u, :, span].astype(jnp.float32)
            slopes = (
                0.5 * (1.0 + lax.erf(pre * root_half))
                + pre * jnp.exp(-0.5 * pre * pre) * gauss_norm
            )
            out[:, span] = (act_buf[u, :, span].astype(jnp.float32) * slopes).astype(jnp.bfloat16)

    for u, pair in loads[:-1]:
        gelu_grad(u, pair, stage.at[u])

    pl.semaphore_wait(barrier, n_gy - 1 + plane - 1)

    def tile_copy(buf, i, ssem, rsem, source):
        return pltpu.make_async_remote_copy(
            src_ref=buf.at[source], dst_ref=buf.at[source],
            send_sem=ssem.at[line_peer(i)], recv_sem=rsem.at[source],
            device_id={"gy": line_peer(i)}, device_id_type=MESH,
        )

    def x_copy(i, source):
        u = lax.rem(g + i, n_gx)
        return pltpu.make_async_remote_copy(
            src_ref=stage.at[u],
            dst_ref=cols.at[p, source],
            send_sem=x_send.at[u], recv_sem=z_recv.at[slot(p, source)],
            device_id={"gx": u}, device_id_type=MESH,
        )

    def z_copy(q, u, step, sems):
        return pltpu.make_async_remote_copy(
            src_ref=cols.at[q, u], dst_ref=cols.at[q, u],
            send_sem=sems.at[slot(q, u)], recv_sem=z_recv.at[slot(q, u)],
            device_id={"gy": lax.rem(p + step + n_gy, n_gy)}, device_id_type=MESH,
        )

    def out_copy(q, u):
        return pltpu.make_async_copy(cols.at[q, u], cols_out.at[u, q], out_sem.at[slot(q, u)])

    def pass_right(q, u):
        @pl.when(p + 1 < n_gy)
        def _():
            z_copy(q, u, 1, right_send).start()

    def pass_left(q, u):
        @pl.when(p >= 1)
        def _():
            z_copy(q, u, -1, left_send).start()

    for i in range(1, n_gx):
        x_copy(i, g).start()
    gelu_grad(loads[-1][0], loads[-1][1], cols.at[p, g])
    pass_right(p, g)
    pass_left(p, g)
    out_copy(p, g).start()

    widened = inputs[...].astype(jnp.float32)
    mean_here = jnp.sum(widened, axis=1, keepdims=True) / width
    centred = widened - mean_here
    square_here = jnp.sum(centred * centred, axis=1, keepdims=True)
    stat_a[p] = to_tile(pad, mean_here, square_here, rows_in)
    for i in range(1, n_gy):
        tile_copy(stat_a, i, stat_send, stat_recv, p).start()

    for i in range(1, n_gx):
        u = lax.rem(g + i, n_gx)
        x_copy(i, u).wait_recv()
        pass_right(p, u)
        pass_left(p, u)
        out_copy(p, u).start()
    for i in range(1, n_gy):
        tile_copy(stat_a, i, stat_send, stat_recv, line_peer(i)).wait_recv()
    columns = [to_columns(pad, stat_a[q], rows_in) for q in range(n_gy)]
    mean = sum(c[0] for c in columns) / n_gy
    total = sum(c[1] + width * (c[0] - mean) * (c[0] - mean) for c in columns)
    inv_std = lax.rsqrt(total / model + epsilon)
    x_hat[...] = (inputs[...].astype(jnp.float32) - mean) * inv_std
    normed_own[...] = (x_hat[...] * row(gain, slice(None)) + row(bias, slice(None))).astype(jnp.bfloat16)

    def norm_copy(i, source):
        other, where = plane_peer(i)
        return pltpu.make_async_remote_copy(
            src_ref=normed_own, dst_ref=normed_out.at[source],
            send_sem=norm_send.at[other], recv_sem=norm_recv.at[source],
            device_id=where, device_id_type=MESH,
        )

    @pl.loop(1, plane)
    def _(i):
        norm_copy(i, me).start()

    norm_own = pltpu.make_async_copy(normed_own, normed_out.at[me], norm_own_sem)
    norm_own.start()

    w_copy.wait()

    def part_copy(q, u, j, source, span):
        owner = q * ratio + j
        return pltpu.make_async_remote_copy(
            src_ref=part_send.at[q, u, j, :, span], dst_ref=part_recv.at[source, :, span],
            send_sem=part_ssem.at[u * n_gz + owner], recv_sem=part_rsem.at[source],
            device_id={"gx": u, "gz": owner}, device_id_type=MESH,
        )

    def multiply(q, units):
        count = n_gx if units is None else 1

        @pl.loop(0, width // SEND)
        def _(c):
            span = pl.ds(pl.multiple_of(c * SEND, SEND), SEND)
            block = cols[q].reshape(n_gx * rows, depth) if units is None else cols[q, units]
            for part in range(0, SEND, CHUNK):
                piece = pl.ds(pl.multiple_of(c * SEND + part, CHUNK), CHUNK)
                value = jnp.dot(block, w_buf[:, piece], preferred_element_type=jnp.float32)
                value = value.astype(jnp.bfloat16).reshape(count, ratio, rows_in, CHUNK)
                if units is None:
                    part_send[q, :, :, :, piece] = value
                else:
                    part_send[q, units, :, :, piece] = value[0]
            for u in range(n_gx) if units is None else [units]:
                for j in range(ratio):
                    mine = jnp.logical_and(u == g, q * ratio + j == t)

                    @pl.when(mine)
                    def _():
                        pltpu.make_async_copy(
                            part_send.at[q, u, j, :, span], part_recv.at[me, :, span], part_own_sem
                        ).start()

                    @pl.when(jnp.logical_not(mine))
                    def _():
                        part_copy(q, u, j, me, span).start()

    multiply(p, None)

    def take(s, k):
        u = lax.rem(g + k, n_gx)

        @pl.when(p - s >= 0)
        def _():
            z_copy(p - s, u, 1, right_send).wait_recv()
            pass_right(p - s, u)
            out_copy(p - s, u).start()

        @pl.when(p + s < n_gy)
        def _():
            z_copy(p + s, u, -1, left_send).wait_recv()
            pass_left(p + s, u)
            out_copy(p + s, u).start()

    @pl.loop(1, n_gy - 1)
    def _(s):
        for k in range(n_gx):
            take(s, k)

        @pl.loop(0, 2)
        def _(side):
            q = p + (2 * side - 1) * s

            @pl.when(jnp.logical_and(q >= 0, q < n_gy))
            def _():
                multiply(q, None)

    @pl.when(jnp.logical_or(p == 0, p == n_gy - 1))
    def _():
        @pl.loop(0, n_gx)
        def _(k):
            take(n_gy - 1, k)
            multiply(n_gy - 1 - p, lax.rem(g + k, n_gx))

    pltpu.make_async_copy(part_send.at[0, 0, 0], part_recv.at[me], part_own_sem).wait()

    @pl.loop(1, plane)
    def _(i):
        other, where = plane_peer(i)
        pltpu.make_async_remote_copy(
            src_ref=part_send.at[0, 0, 0], dst_ref=part_recv.at[other],
            send_sem=part_ssem.at[other], recv_sem=part_rsem.at[other],
            device_id=where, device_id_type=MESH,
        ).wait_recv()

    row_sum = jnp.zeros((rows_in, 1), jnp.float32)
    row_dot = jnp.zeros((rows_in, 1), jnp.float32)
    for start in range(0, width, CHUNK):
        span = slice(start, start + CHUNK)
        block = lax.fori_loop(
            0, plane,
            lambda i, acc: acc + part_recv[i, :, span].astype(jnp.float32),
            jnp.zeros((rows_in, CHUNK), jnp.float32),
            unroll=8,
        )
        grad_normed[:, span] = block
        hat = x_hat[:, span]
        sums[me, 0:1, span] = jnp.sum(block * hat, axis=0, keepdims=True)
        sums[me, 1:2, span] = jnp.sum(block, axis=0, keepdims=True)
        scaled = block * row(gain, span)
        row_sum = row_sum + jnp.sum(scaled, axis=1, keepdims=True)
        row_dot = row_dot + jnp.sum(scaled * hat, axis=1, keepdims=True)
    stat_b[p] = to_tile(pad, row_sum, row_dot, rows_in)
    for i in range(1, n_gy):
        tile_copy(stat_b, i, last_send, last_recv, p).start()

    def sums_copy(i, source):
        other, where = plane_peer(i)
        return pltpu.make_async_remote_copy(
            src_ref=sums.at[source], dst_ref=sums.at[source],
            send_sem=sums_send.at[other], recv_sem=sums_recv.at[source],
            device_id=where, device_id_type=MESH,
        )

    @pl.loop(1, plane)
    def _(i):
        sums_copy(i, me).start()

    for i in range(1, n_gy):
        tile_copy(stat_b, i, last_send, last_recv, line_peer(i)).wait_recv()
    both = stat_b[0]
    for q in range(1, n_gy):
        both = both + stat_b[q]
    grad_sum, grad_dot = to_columns(pad, both, rows_in)
    for start in range(0, width, CHUNK):
        span = slice(start, start + CHUNK)
        scaled = grad_normed[:, span] * row(gain, span)
        grad_inputs[:, span] = (
            inv_std * (scaled - grad_sum / model - x_hat[:, span] * (grad_dot / model))
        ).astype(jnp.bfloat16)

    @pl.loop(1, plane)
    def _(i):
        sums_copy(i, plane_peer(i)[0]).wait_recv()

    both = lax.fori_loop(
        0, plane, lambda i, acc: acc + sums[i], jnp.zeros((2, width), jnp.float32), unroll=8
    )
    grad_gain[...] = both[0]
    grad_bias[...] = both[1]

    norm_own.wait()

    @pl.loop(1, plane)
    def _(i):
        other, where = plane_peer(i)
        norm_copy(i, me).wait_send()
        norm_copy(i, other).wait_recv()
        sums_copy(i, me).wait_send()
        pltpu.make_async_remote_copy(
            src_ref=part_send.at[0, 0, 0], dst_ref=part_recv.at[me],
            send_sem=part_ssem.at[other], recv_sem=part_rsem.at[me],
            device_id=where, device_id_type=MESH,
        ).wait_send()

    for i in range(1, n_gy):
        tile_copy(stat_a, i, stat_send, stat_recv, p).wait_send()
        tile_copy(stat_b, i, last_send, last_recv, p).wait_send()
    for i in range(1, n_gx):
        x_copy(i, g).wait_send()

    @pl.loop(0, n_gy)
    def _(q):
        for u in range(n_gx):
            out_copy(q, u).wait()

            @pl.when(jnp.logical_and(q <= p, p + 1 < n_gy))
            def _():
                z_copy(q, u, 1, right_send).wait_send()

            @pl.when(jnp.logical_and(q >= p, p >= 1))
            def _():
                z_copy(q, u, -1, left_send).wait_send()


def on_device(shape, inputs, norm_gain, norm_bias, pre_act, grad_act, up_weight):
    n_gx, n_gy, n_gz = shape["gx"], shape["gy"], shape["gz"]
    plane = n_gx * n_gz
    rows_in, width = inputs.shape
    rows = pre_act.shape[0]
    depth = up_weight.shape[1]
    ratio = rows // rows_in
    whole, vmem = pl.BlockSpec(memory_space=pl.ANY), pl.BlockSpec(memory_space=pltpu.VMEM)
    dma = pltpu.SemaphoreType.DMA
    bf16, f32 = jnp.bfloat16, jnp.float32
    slots = n_gx * n_gy
    grad_cols, normed_all, grad_inputs, grad_gain, grad_bias = pl.pallas_call(
        functools.partial(kernel, (n_gx, n_gy, n_gz, rows, rows_in, width, depth)),
        out_shape=(
            jax.ShapeDtypeStruct((n_gx, n_gy, rows, depth), bf16),
            jax.ShapeDtypeStruct((plane, rows_in, width), bf16),
            jax.ShapeDtypeStruct((rows_in, width), bf16),
            jax.ShapeDtypeStruct((width,), f32),
            jax.ShapeDtypeStruct((width,), f32),
        ),
        in_specs=[vmem, vmem, vmem, whole, whole, whole],
        out_specs=(whole, whole, vmem, vmem, vmem),
        scratch_shapes=[
            pltpu.VMEM((n_gx, rows, depth), bf16),
            pltpu.VMEM((n_gx, rows, depth), bf16),
            pltpu.VMEM((n_gx, rows, depth), bf16),
            pltpu.VMEM((depth, width), bf16),
            pltpu.VMEM((n_gy, n_gx, rows, depth), bf16),
            pltpu.VMEM((n_gy, n_gx, ratio, rows_in, width), bf16),
            pltpu.VMEM((plane, rows_in, width), bf16),
            pltpu.VMEM((rows_in, width), f32),
            pltpu.VMEM((rows_in, width), f32),
            pltpu.VMEM((rows_in, width), bf16),
            pltpu.VMEM((plane, 2, width), f32),
            pltpu.VMEM((LANES, LANES), f32),
            pltpu.VMEM((n_gy, SUB, LANES), f32),
            pltpu.VMEM((n_gy, SUB, LANES), f32),
            dma((n_gx,)), dma((n_gx,)), dma, dma((slots,)), dma((slots,)), dma((slots,)), dma((slots,)), dma((n_gx,)),
            dma((n_gy,)), dma((n_gy,)), dma((plane,)), dma((plane,)), dma,
            dma((plane,)), dma((plane,)), dma,
            dma((plane,)), dma((plane,)), dma((n_gy,)), dma((n_gy,)),
        ],
        compiler_params=pltpu.CompilerParams(
            collective_id=0, has_side_effects=True, vmem_limit_bytes=60 * 1024 * 1024
        ),
    )(inputs, norm_gain, norm_bias, pre_act, grad_act, up_weight[0])
    tokens = slots * rows
    weight_block = lax.dot_general(
        grad_cols.reshape(tokens, depth),
        normed_all.reshape(tokens, width),
        (((0,), (0,)), ((), ())),
        preferred_element_type=jnp.float32,
    )
    return grad_inputs, grad_gain, grad_bias, weight_block.reshape(up_weight.shape)


def solution(mesh):
    in_specs = (
        P(("gx", "gz"), "gy"),
        P("gy"),
        P("gy"),
        P(("gx", "gy"), "gz"),
        P(("gx", "gy"), "gz"),
        P("gz", "gx", "gy"),
    )
    out_specs = (P(("gx", "gz"), "gy"), P("gy"), P("gy"), P("gz", "gx", "gy"))
    return jax.shard_map(
        functools.partial(on_device, dict(mesh.shape)),
        mesh=mesh, in_specs=in_specs, out_specs=out_specs, check_vma=False,
    )
```

```python
import functools

import jax
import jax.numpy as jnp
from jax import lax
from jax.experimental import pallas as pl
from jax.experimental.pallas import tpu as pltpu
from jax.sharding import PartitionSpec as P

MESH = pl.DeviceIdType.MESH
LANES = 128
SUB = 8
CHUNK = 256
SEND = 512

epsilon = 1e-05
root_half = 0.7071067811865476
gauss_norm = 0.3989422804014327


def to_tile(pad, first, second, rows):
    lane = lax.broadcasted_iota(jnp.int32, (rows, LANES), 1)
    pad[...] = jnp.zeros_like(pad)
    pad[:rows, :] = jnp.where(lane == 0, first, jnp.where(lane == 1, second, 0.0))
    return pad[...].T[:SUB, :]


def to_columns(pad, tile, rows):
    pad[...] = jnp.zeros_like(pad)
    pad[:SUB, :] = tile
    flipped = pad[...].T
    return flipped[:rows, 0:1], flipped[:rows, 1:2]


def kernel(
    sizes,
    inputs, gain, bias, pre_act, grad_act, weight,
    cols_out, normed_out, grad_inputs, grad_sums,
    pre_buf, act_buf, stage, w_buf, cols, acc, part_send, part_recv, x_hat, grad_normed, normed_own, sums, pad, stat_a, stat_b,
    pre_sem, act_sem, w_sem, out_sem, z_recv, right_send, left_send, x_send,
    stat_send, stat_recv, norm_send, norm_recv, norm_own_sem, part_ssem, part_rsem, part_own_sem,
    sums_send, sums_recv, last_send, last_recv,
):
    n_gx, n_gy, n_gz, rows, rows_in, width, depth, parts = sizes
    deep = depth // parts
    ratio = rows // rows_in
    plane = n_gx * n_gz
    g, p, t = lax.axis_index("gx"), lax.axis_index("gy"), lax.axis_index("gz")
    me = g * n_gz + t
    model = width * n_gy

    def line_peer(i):
        return lax.rem(p + i, n_gy)

    def plane_peer(i):
        other = lax.rem(me + i, plane)
        return other, {"gx": other // n_gz, "gz": lax.rem(other, n_gz)}

    def slot(q, u):
        return q * n_gx + u

    def row(ref, span):
        return ref[span].reshape(1, -1)

    barrier = pltpu.get_barrier_semaphore()
    for i in range(1, n_gy):
        pl.semaphore_signal(barrier, inc=1, device_id={"gy": line_peer(i)}, device_id_type=MESH)

    @pl.loop(1, plane)
    def _(i):
        pl.semaphore_signal(barrier, inc=1, device_id=plane_peer(i)[1], device_id_type=MESH)

    def deep_span(h, base=0):
        return pl.ds(pl.multiple_of(base + h * deep, LANES), deep)

    def load(u, h):
        source = deep_span(h, u * depth)
        return (
            pltpu.make_async_copy(
                pre_act.at[:, source], pre_buf.at[u, :, deep_span(h)], pre_sem.at[u * parts + h]
            ),
            pltpu.make_async_copy(
                grad_act.at[:, source], act_buf.at[u, :, deep_span(h)], act_sem.at[u * parts + h]
            ),
        )

    order = [lax.rem(g + i, n_gx) for i in list(range(1, n_gx)) + [0]]
    for h in range(parts):
        for u in order:
            for copy in load(u, h):
                copy.start()
    w_copy = pltpu.make_async_copy(weight, w_buf, w_sem)
    w_copy.start()

    step = next(n for n in (384, 256, LANES) if deep % n == 0)

    def gelu_grad(u, h, out):
        for copy in load(u, h):
            copy.wait()

        @pl.loop(0, deep // step)
        def _(c):
            span = pl.ds(pl.multiple_of(h * deep + c * step, LANES), step)
            pre = pre_buf[u, :, span].astype(jnp.float32)
            slopes = (
                0.5 * (1.0 + lax.erf(pre * root_half))
                + pre * jnp.exp(-0.5 * pre * pre) * gauss_norm
            )
            out[:, span] = (act_buf[u, :, span].astype(jnp.float32) * slopes).astype(jnp.bfloat16)

    def tile_copy(buf, i, ssem, rsem, source):
        return pltpu.make_async_remote_copy(
            src_ref=buf.at[source], dst_ref=buf.at[source],
            send_sem=ssem.at[line_peer(i)], recv_sem=rsem.at[source],
            device_id={"gy": line_peer(i)}, device_id_type=MESH,
        )

    def x_copy(i, source, h):
        u = lax.rem(g + i, n_gx)
        return pltpu.make_async_remote_copy(
            src_ref=stage.at[u, :, deep_span(h)],
            dst_ref=cols.at[p, source, :, deep_span(h)],
            send_sem=x_send.at[u], recv_sem=z_recv.at[slot(p, source) * parts + h],
            device_id={"gx": u}, device_id_type=MESH,
        )

    def z_copy(q, u, h, step, sems):
        return pltpu.make_async_remote_copy(
            src_ref=cols.at[q, u, :, deep_span(h)], dst_ref=cols.at[q, u, :, deep_span(h)],
            send_sem=sems.at[slot(q, u)], recv_sem=z_recv.at[slot(q, u) * parts + h],
            device_id={"gy": lax.rem(p + step + n_gy, n_gy)}, device_id_type=MESH,
        )

    def out_copy(q, u):
        return pltpu.make_async_copy(cols.at[q, u], cols_out.at[u, q], out_sem.at[slot(q, u)])

    def pass_right(q, u, h):
        @pl.when(p + 1 < n_gy)
        def _():
            z_copy(q, u, h, 1, right_send).start()

    def pass_left(q, u, h):
        @pl.when(p >= 1)
        def _():
            z_copy(q, u, h, -1, left_send).start()

    for h in range(parts):
        for i in range(1, n_gx):
            u = lax.rem(g + i, n_gx)
            gelu_grad(u, h, stage.at[u])
            if h == 0 and i == 1:
                pl.semaphore_wait(barrier, n_gy - 1 + plane - 1)
            x_copy(i, g, h).start()
        gelu_grad(g, h, cols.at[p, g])
        pass_right(p, g, h)
        pass_left(p, g, h)
    out_copy(p, g).start()

    widened = inputs[...].astype(jnp.float32)
    mean_here = jnp.sum(widened, axis=1, keepdims=True) / width
    centred = widened - mean_here
    square_here = jnp.sum(centred * centred, axis=1, keepdims=True)
    stat_a[p] = to_tile(pad, mean_here, square_here, rows_in)
    for i in range(1, n_gy):
        tile_copy(stat_a, i, stat_send, stat_recv, p).start()

    for i in range(1, n_gx):
        u = lax.rem(g + i, n_gx)

        @pl.loop(0, parts)
        def _(h):
            x_copy(i, u, h).wait_recv()
            pass_right(p, u, h)
            pass_left(p, u, h)

        out_copy(p, u).start()
    for i in range(1, n_gy):
        tile_copy(stat_a, i, stat_send, stat_recv, line_peer(i)).wait_recv()
    columns = [to_columns(pad, stat_a[q], rows_in) for q in range(n_gy)]
    mean = sum(c[0] for c in columns) / n_gy
    total = sum(c[1] + width * (c[0] - mean) * (c[0] - mean) for c in columns)
    inv_std = lax.rsqrt(total / model + epsilon)
    x_hat[...] = (inputs[...].astype(jnp.float32) - mean) * inv_std
    normed_own[...] = (x_hat[...] * row(gain, slice(None)) + row(bias, slice(None))).astype(jnp.bfloat16)

    def norm_copy(i, source):
        other, where = plane_peer(i)
        return pltpu.make_async_remote_copy(
            src_ref=normed_own, dst_ref=normed_out.at[source],
            send_sem=norm_send.at[other], recv_sem=norm_recv.at[source],
            device_id=where, device_id_type=MESH,
        )

    @pl.loop(1, plane)
    def _(i):
        norm_copy(i, me).start()

    norm_own = pltpu.make_async_copy(normed_own, normed_out.at[me], norm_own_sem)
    norm_own.start()

    w_copy.wait()

    def part_copy(q, u, j, source, span):
        owner = q * ratio + j
        return pltpu.make_async_remote_copy(
            src_ref=part_send.at[q, u, j, :, span], dst_ref=part_recv.at[source, :, span],
            send_sem=part_ssem.at[u * n_gz + owner], recv_sem=part_rsem.at[source],
            device_id={"gx": u, "gz": owner}, device_id_type=MESH,
        )

    def send_parts(q, u, span):
        for j in range(ratio):
            mine = jnp.logical_and(u == g, q * ratio + j == t)

            @pl.when(mine)
            def _():
                pltpu.make_async_copy(
                    part_send.at[q, u, j, :, span], part_recv.at[me, :, span], part_own_sem
                ).start()

            @pl.when(jnp.logical_not(mine))
            def _():
                part_copy(q, u, j, me, span).start()

    def multiply(q):
        @pl.loop(0, width // SEND)
        def _(c):
            for part in range(0, SEND, CHUNK):
                piece = pl.ds(pl.multiple_of(c * SEND + part, CHUNK), CHUNK)
                block = cols[q].reshape(n_gx * rows, depth)
                value = jnp.dot(block, w_buf[:, piece], preferred_element_type=jnp.float32)
                part_send[q, :, :, :, piece] = value.astype(jnp.bfloat16).reshape(
                    n_gx, ratio, rows_in, CHUNK
                )
            for u in range(n_gx):
                send_parts(q, u, pl.ds(pl.multiple_of(c * SEND, SEND), SEND))

    multiply(p)

    def take(s, u, h):
        @pl.when(p - s >= 0)
        def _():
            z_copy(p - s, u, h, 1, right_send).wait_recv()
            pass_right(p - s, u, h)

        @pl.when(p + s < n_gy)
        def _():
            z_copy(p + s, u, h, -1, left_send).wait_recv()
            pass_left(p + s, u, h)

    @pl.loop(1, n_gy - 1)
    def _(s):
        @pl.loop(0, n_gx * parts)
        def _(k):
            take(s, lax.rem(g + k // parts, n_gx), lax.rem(k, parts))

        @pl.loop(0, 2)
        def _(side):
            q = p + (2 * side - 1) * s

            @pl.when(jnp.logical_and(q >= 0, q < n_gy))
            def _():
                for u in range(n_gx):
                    out_copy(q, u).start()
                multiply(q)

    @pl.when(jnp.logical_or(p == 0, p == n_gy - 1))
    def _():
        q = n_gy - 1 - p

        @pl.loop(0, n_gx)
        def _(k):
            u = lax.rem(g + k, n_gx)
            acc[...] = jnp.zeros_like(acc)

            @pl.loop(0, parts - 1)
            def _(h):
                take(n_gy - 1, u, h)

                @pl.loop(0, width // CHUNK)
                def _(c):
                    piece = pl.ds(pl.multiple_of(c * CHUNK, CHUNK), CHUNK)
                    acc[:, piece] += jnp.dot(
                        cols[q, u, :, deep_span(h)], w_buf[deep_span(h), piece],
                        preferred_element_type=jnp.float32,
                    )

            take(n_gy - 1, u, parts - 1)
            out_copy(q, u).start()
            last = deep_span(parts - 1)

            @pl.loop(0, width // SEND)
            def _(c):
                for part in range(0, SEND, CHUNK):
                    piece = pl.ds(pl.multiple_of(c * SEND + part, CHUNK), CHUNK)
                    value = acc[:, piece] + jnp.dot(
                        cols[q, u, :, last], w_buf[last, piece], preferred_element_type=jnp.float32
                    )
                    part_send[q, u, :, :, piece] = value.astype(jnp.bfloat16).reshape(
                        ratio, rows_in, CHUNK
                    )
                send_parts(q, u, pl.ds(pl.multiple_of(c * SEND, SEND), SEND))

    pltpu.make_async_copy(part_send.at[0, 0, 0], part_recv.at[me], part_own_sem).wait()

    @pl.loop(1, plane)
    def _(i):
        other, where = plane_peer(i)
        pltpu.make_async_remote_copy(
            src_ref=part_send.at[0, 0, 0], dst_ref=part_recv.at[other],
            send_sem=part_ssem.at[other], recv_sem=part_rsem.at[other],
            device_id=where, device_id_type=MESH,
        ).wait_recv()

    row_sum = jnp.zeros((rows_in, 1), jnp.float32)
    row_dot = jnp.zeros((rows_in, 1), jnp.float32)
    for start in range(0, width, CHUNK):
        span = slice(start, start + CHUNK)
        block = lax.fori_loop(
            0, plane,
            lambda i, acc: acc + part_recv[i, :, span].astype(jnp.float32),
            jnp.zeros((rows_in, CHUNK), jnp.float32),
            unroll=8,
        )
        grad_normed[:, span] = block
        hat = x_hat[:, span]
        sums[me, 0:1, span] = jnp.sum(block * hat, axis=0, keepdims=True)
        sums[me, 1:2, span] = jnp.sum(block, axis=0, keepdims=True)
        scaled = block * row(gain, span)
        row_sum = row_sum + jnp.sum(scaled, axis=1, keepdims=True)
        row_dot = row_dot + jnp.sum(scaled * hat, axis=1, keepdims=True)
    stat_b[p] = to_tile(pad, row_sum, row_dot, rows_in)
    for i in range(1, n_gy):
        tile_copy(stat_b, i, last_send, last_recv, p).start()

    def sums_copy(i, source):
        other, where = plane_peer(i)
        return pltpu.make_async_remote_copy(
            src_ref=sums.at[source], dst_ref=sums.at[source],
            send_sem=sums_send.at[other], recv_sem=sums_recv.at[source],
            device_id=where, device_id_type=MESH,
        )

    @pl.loop(1, plane)
    def _(i):
        sums_copy(i, me).start()

    for i in range(1, n_gy):
        tile_copy(stat_b, i, last_send, last_recv, line_peer(i)).wait_recv()
    both = stat_b[0]
    for q in range(1, n_gy):
        both = both + stat_b[q]
    grad_sum, grad_dot = to_columns(pad, both, rows_in)
    for start in range(0, width, CHUNK):
        span = slice(start, start + CHUNK)
        scaled = grad_normed[:, span] * row(gain, span)
        grad_inputs[:, span] = (
            inv_std * (scaled - grad_sum / model - x_hat[:, span] * (grad_dot / model))
        ).astype(jnp.bfloat16)

    @pl.loop(1, plane)
    def _(i):
        sums_copy(i, plane_peer(i)[0]).wait_recv()

    grad_sums[...] = lax.fori_loop(
        0, plane, lambda i, acc: acc + sums[i], jnp.zeros((2, width), jnp.float32), unroll=8
    )

    norm_own.wait()

    @pl.loop(1, plane)
    def _(i):
        other, where = plane_peer(i)
        norm_copy(i, me).wait_send()
        norm_copy(i, other).wait_recv()
        sums_copy(i, me).wait_send()
        pltpu.make_async_remote_copy(
            src_ref=part_send.at[0, 0, 0], dst_ref=part_recv.at[me],
            send_sem=part_ssem.at[other], recv_sem=part_rsem.at[me],
            device_id=where, device_id_type=MESH,
        ).wait_send()

    for i in range(1, n_gy):
        tile_copy(stat_a, i, stat_send, stat_recv, p).wait_send()
        tile_copy(stat_b, i, last_send, last_recv, p).wait_send()
    for i in range(1, n_gx):
        u = lax.rem(g + i, n_gx)
        pltpu.make_async_remote_copy(
            src_ref=stage.at[u], dst_ref=cols.at[p, g],
            send_sem=x_send.at[u], recv_sem=z_recv.at[0],
            device_id={"gx": u}, device_id_type=MESH,
        ).wait_send()

    def sent(q, u, step, sems):
        return pltpu.make_async_remote_copy(
            src_ref=cols.at[q, u], dst_ref=cols.at[q, u],
            send_sem=sems.at[slot(q, u)], recv_sem=z_recv.at[0],
            device_id={"gy": lax.rem(p + step + n_gy, n_gy)}, device_id_type=MESH,
        )

    @pl.loop(0, n_gy)
    def _(q):
        for u in range(n_gx):
            out_copy(q, u).wait()

            @pl.when(jnp.logical_and(q <= p, p + 1 < n_gy))
            def _():
                sent(q, u, 1, right_send).wait_send()

            @pl.when(jnp.logical_and(q >= p, p >= 1))
            def _():
                sent(q, u, -1, left_send).wait_send()


def on_device(shape, inputs, norm_gain, norm_bias, pre_act, grad_act, up_weight):
    n_gx, n_gy, n_gz = shape["gx"], shape["gy"], shape["gz"]
    plane = n_gx * n_gz
    rows_in, width = inputs.shape
    rows = pre_act.shape[0]
    depth = up_weight.shape[1]
    parts = next(n for n in (4, 3, 2, 1) if depth % (n * LANES) == 0)
    whole, vmem = pl.BlockSpec(memory_space=pl.ANY), pl.BlockSpec(memory_space=pltpu.VMEM)
    dma = pltpu.SemaphoreType.DMA
    bf16, f32 = jnp.bfloat16, jnp.float32
    ratio = rows // rows_in
    slots = n_gx * n_gy
    grad_cols, normed_all, grad_inputs, grad_sums = pl.pallas_call(
        functools.partial(kernel, (n_gx, n_gy, n_gz, rows, rows_in, width, depth, parts)),
        out_shape=(
            jax.ShapeDtypeStruct((n_gx, n_gy, rows, depth), bf16),
            jax.ShapeDtypeStruct((plane, rows_in, width), bf16),
            jax.ShapeDtypeStruct((rows_in, width), bf16),
            jax.ShapeDtypeStruct((2, width), f32),
        ),
        in_specs=[vmem, vmem, vmem, whole, whole, whole],
        out_specs=(whole, whole, vmem, vmem),
        scratch_shapes=[
            pltpu.VMEM((n_gx, rows, depth), bf16),
            pltpu.VMEM((n_gx, rows, depth), bf16),
            pltpu.VMEM((n_gx, rows, depth), bf16),
            pltpu.VMEM((depth, width), bf16),
            pltpu.VMEM((n_gy, n_gx, rows, depth), bf16),
            pltpu.VMEM((rows, width), f32),
            pltpu.VMEM((n_gy, n_gx, ratio, rows_in, width), bf16),
            pltpu.VMEM((plane, rows_in, width), bf16),
            pltpu.VMEM((rows_in, width), f32),
            pltpu.VMEM((rows_in, width), f32),
            pltpu.VMEM((rows_in, width), bf16),
            pltpu.VMEM((plane, 2, width), f32),
            pltpu.VMEM((LANES, LANES), f32),
            pltpu.VMEM((n_gy, SUB, LANES), f32),
            pltpu.VMEM((n_gy, SUB, LANES), f32),
            dma((n_gx * parts,)), dma((n_gx * parts,)), dma, dma((slots,)), dma((slots * parts,)), dma((slots,)), dma((slots,)), dma((n_gx,)),
            dma((n_gy,)), dma((n_gy,)), dma((plane,)), dma((plane,)), dma,
            dma((plane,)), dma((plane,)), dma,
            dma((plane,)), dma((plane,)), dma((n_gy,)), dma((n_gy,)),
        ],
        compiler_params=pltpu.CompilerParams(
            collective_id=0, has_side_effects=True, vmem_limit_bytes=60 * 1024 * 1024
        ),
    )(inputs, norm_gain, norm_bias, pre_act, grad_act, up_weight[0])
    tokens = slots * rows
    weight_block = lax.dot_general(
        grad_cols.reshape(tokens, depth),
        normed_all.reshape(tokens, width),
        (((0,), (0,)), ((), ())),
        preferred_element_type=jnp.float32,
    )
    return grad_inputs, grad_sums[0], grad_sums[1], weight_block.reshape(up_weight.shape)


def solution(mesh):
    in_specs = (
        P(("gx", "gz"), "gy"),
        P("gy"),
        P("gy"),
        P(("gx", "gy"), "gz"),
        P(("gx", "gy"), "gz"),
        P("gz", "gx", "gy"),
    )
    out_specs = (P(("gx", "gz"), "gy"), P("gy"), P("gy"), P("gz", "gx", "gy"))
    return jax.shard_map(
        functools.partial(on_device, dict(mesh.shape)),
        mesh=mesh, in_specs=in_specs, out_specs=out_specs, check_vma=False,
    )
```

```python
import functools

import jax
import jax.numpy as jnp
from jax import lax
from jax.experimental import pallas as pl
from jax.experimental.pallas import tpu as pltpu
from jax.sharding import PartitionSpec as P

MESH = pl.DeviceIdType.MESH
LANES = 128
SUB = 8
CHUNK = 256
SEND = 512

epsilon = 1e-05
root_half = 0.7071067811865476
gauss_norm = 0.3989422804014327


def to_tile(pad, first, second, rows):
    lane = lax.broadcasted_iota(jnp.int32, (rows, LANES), 1)
    pad[...] = jnp.zeros_like(pad)
    pad[:rows, :] = jnp.where(lane == 0, first, jnp.where(lane == 1, second, 0.0))
    return pad[...].T[:SUB, :]


def to_columns(pad, tile, rows):
    pad[...] = jnp.zeros_like(pad)
    pad[:SUB, :] = tile
    flipped = pad[...].T
    return flipped[:rows, 0:1], flipped[:rows, 1:2]


def kernel(
    sizes,
    inputs, gain, bias, pre_act, grad_act, weight,
    cols_out, normed_out, grad_inputs, grad_sums,
    pre_buf, act_buf, stage, w_buf, cols, acc, part_send, part_recv, x_hat, grad_normed, normed_own, sums, pad, stat_a, stat_b,
    pre_sem, act_sem, w_sem, out_sem, z_recv, right_send, left_send, x_send,
    stat_send, stat_recv, norm_send, norm_recv, norm_own_sem, part_ssem, part_rsem, part_own_sem,
    sums_send, sums_recv, last_send, last_recv,
):
    n_gx, n_gy, n_gz, rows, rows_in, width, depth, parts = sizes
    deep = depth // parts
    ratio = rows // rows_in
    plane = n_gx * n_gz
    g, p, t = lax.axis_index("gx"), lax.axis_index("gy"), lax.axis_index("gz")
    me = g * n_gz + t
    model = width * n_gy

    def line_peer(i):
        return lax.rem(p + i, n_gy)

    def plane_peer(i):
        other = lax.rem(me + i, plane)
        return other, {"gx": other // n_gz, "gz": lax.rem(other, n_gz)}

    def slot(q, u):
        return q * n_gx + u

    def row(ref, span):
        return ref[span].reshape(1, -1)

    barrier = pltpu.get_barrier_semaphore()
    for i in range(1, n_gy):
        pl.semaphore_signal(barrier, inc=1, device_id={"gy": line_peer(i)}, device_id_type=MESH)

    @pl.loop(1, plane)
    def _(i):
        pl.semaphore_signal(barrier, inc=1, device_id=plane_peer(i)[1], device_id_type=MESH)

    def deep_span(h, base=0):
        return pl.ds(pl.multiple_of(base + h * deep, LANES), deep)

    def load(u, h):
        source = deep_span(h, u * depth)
        return (
            pltpu.make_async_copy(
                pre_act.at[:, source], pre_buf.at[u, :, deep_span(h)], pre_sem.at[u * parts + h]
            ),
            pltpu.make_async_copy(
                grad_act.at[:, source], act_buf.at[u, :, deep_span(h)], act_sem.at[u * parts + h]
            ),
        )

    order = [lax.rem(g + i, n_gx) for i in list(range(1, n_gx)) + [0]]
    for h in range(parts):
        for u in order:
            for copy in load(u, h):
                copy.start()
    w_copy = pltpu.make_async_copy(weight, w_buf, w_sem)
    w_copy.start()

    step = next(n for n in (384, 256, LANES) if deep % n == 0)

    def gelu_grad(u, h, out):
        for copy in load(u, h):
            copy.wait()

        @pl.loop(0, deep // step)
        def _(c):
            span = pl.ds(pl.multiple_of(h * deep + c * step, LANES), step)
            pre = pre_buf[u, :, span].astype(jnp.float32)
            slopes = (
                0.5 * (1.0 + lax.erf(pre * root_half))
                + pre * jnp.exp(-0.5 * pre * pre) * gauss_norm
            )
            out[:, span] = (act_buf[u, :, span].astype(jnp.float32) * slopes).astype(jnp.bfloat16)

    def tile_copy(buf, i, ssem, rsem, source):
        return pltpu.make_async_remote_copy(
            src_ref=buf.at[source], dst_ref=buf.at[source],
            send_sem=ssem.at[line_peer(i)], recv_sem=rsem.at[source],
            device_id={"gy": line_peer(i)}, device_id_type=MESH,
        )

    def x_copy(i, source, h):
        u = lax.rem(g + i, n_gx)
        return pltpu.make_async_remote_copy(
            src_ref=stage.at[u, :, deep_span(h)],
            dst_ref=cols.at[p, source, :, deep_span(h)],
            send_sem=x_send.at[u], recv_sem=z_recv.at[slot(p, source) * parts + h],
            device_id={"gx": u}, device_id_type=MESH,
        )

    def z_copy(q, u, h, step, sems):
        return pltpu.make_async_remote_copy(
            src_ref=cols.at[q, u, :, deep_span(h)], dst_ref=cols.at[q, u, :, deep_span(h)],
            send_sem=sems.at[slot(q, u)], recv_sem=z_recv.at[slot(q, u) * parts + h],
            device_id={"gy": lax.rem(p + step + n_gy, n_gy)}, device_id_type=MESH,
        )

    def out_copy(q, u):
        return pltpu.make_async_copy(cols.at[q, u], cols_out.at[u, q], out_sem.at[slot(q, u)])

    def pass_right(q, u, h):
        @pl.when(p + 1 < n_gy)
        def _():
            z_copy(q, u, h, 1, right_send).start()

    def pass_left(q, u, h):
        @pl.when(p >= 1)
        def _():
            z_copy(q, u, h, -1, left_send).start()

    for h in range(parts):
        for i in range(1, n_gx):
            u = lax.rem(g + i, n_gx)
            gelu_grad(u, h, stage.at[u])
            if h == 0 and i == 1:
                pl.semaphore_wait(barrier, n_gy - 1 + plane - 1)
            x_copy(i, g, h).start()
        gelu_grad(g, h, cols.at[p, g])
        pass_right(p, g, h)
        pass_left(p, g, h)
    out_copy(p, g).start()

    widened = inputs[...].astype(jnp.float32)
    mean_here = jnp.sum(widened, axis=1, keepdims=True) / width
    centred = widened - mean_here
    square_here = jnp.sum(centred * centred, axis=1, keepdims=True)
    stat_a[p] = to_tile(pad, mean_here, square_here, rows_in)
    for i in range(1, n_gy):
        tile_copy(stat_a, i, stat_send, stat_recv, p).start()

    for i in range(1, n_gx):
        u = lax.rem(g + i, n_gx)

        @pl.loop(0, parts)
        def _(h):
            x_copy(i, u, h).wait_recv()
            pass_right(p, u, h)
            pass_left(p, u, h)

        out_copy(p, u).start()
    for i in range(1, n_gy):
        tile_copy(stat_a, i, stat_send, stat_recv, line_peer(i)).wait_recv()
    columns = [to_columns(pad, stat_a[q], rows_in) for q in range(n_gy)]
    mean = sum(c[0] for c in columns) / n_gy
    total = sum(c[1] + width * (c[0] - mean) * (c[0] - mean) for c in columns)
    inv_std = lax.rsqrt(total / model + epsilon)
    x_hat[...] = (inputs[...].astype(jnp.float32) - mean) * inv_std
    normed_own[...] = (x_hat[...] * row(gain, slice(None)) + row(bias, slice(None))).astype(jnp.bfloat16)

    def norm_copy(i, source):
        other, where = plane_peer(i)
        return pltpu.make_async_remote_copy(
            src_ref=normed_own, dst_ref=normed_out.at[source],
            send_sem=norm_send.at[other], recv_sem=norm_recv.at[source],
            device_id=where, device_id_type=MESH,
        )

    @pl.loop(1, plane)
    def _(i):
        norm_copy(i, me).start()

    norm_own = pltpu.make_async_copy(normed_own, normed_out.at[me], norm_own_sem)
    norm_own.start()

    w_copy.wait()

    def part_copy(q, u, j, source, span):
        owner = q * ratio + j
        return pltpu.make_async_remote_copy(
            src_ref=part_send.at[q, u, j, :, span], dst_ref=part_recv.at[source, :, span],
            send_sem=part_ssem.at[u * n_gz + owner], recv_sem=part_rsem.at[source],
            device_id={"gx": u, "gz": owner}, device_id_type=MESH,
        )

    def send_parts(q, u, span):
        for j in range(ratio):
            mine = jnp.logical_and(u == g, q * ratio + j == t)

            @pl.when(mine)
            def _():
                pltpu.make_async_copy(
                    part_send.at[q, u, j, :, span], part_recv.at[me, :, span], part_own_sem
                ).start()

            @pl.when(jnp.logical_not(mine))
            def _():
                part_copy(q, u, j, me, span).start()

    def multiply(q):
        @pl.loop(0, width // SEND)
        def _(c):
            for part in range(0, SEND, CHUNK):
                piece = pl.ds(pl.multiple_of(c * SEND + part, CHUNK), CHUNK)
                block = cols[q].reshape(n_gx * rows, depth)
                value = jnp.dot(block, w_buf[:, piece], preferred_element_type=jnp.float32)
                part_send[q, :, :, :, piece] = value.astype(jnp.bfloat16).reshape(
                    n_gx, ratio, rows_in, CHUNK
                )
            for u in range(n_gx):
                send_parts(q, u, pl.ds(pl.multiple_of(c * SEND, SEND), SEND))

    multiply(p)

    def take(s, u, h):
        @pl.when(p - s >= 0)
        def _():
            z_copy(p - s, u, h, 1, right_send).wait_recv()
            pass_right(p - s, u, h)

        @pl.when(p + s < n_gy)
        def _():
            z_copy(p + s, u, h, -1, left_send).wait_recv()
            pass_left(p + s, u, h)

    @pl.loop(1, n_gy - 1)
    def _(s):
        @pl.loop(0, n_gx * parts)
        def _(k):
            take(s, lax.rem(g + k // parts, n_gx), lax.rem(k, parts))

        @pl.loop(0, 2)
        def _(side):
            q = p + (2 * side - 1) * s

            @pl.when(jnp.logical_and(q >= 0, q < n_gy))
            def _():
                for u in range(n_gx):
                    out_copy(q, u).start()
                multiply(q)

    @pl.when(jnp.logical_or(p == 0, p == n_gy - 1))
    def _():
        q = n_gy - 1 - p

        @pl.loop(0, n_gx)
        def _(k):
            u = lax.rem(g + k, n_gx)
            acc[...] = jnp.zeros_like(acc)

            @pl.loop(0, parts - 1)
            def _(h):
                take(n_gy - 1, u, h)

                @pl.loop(0, width // CHUNK)
                def _(c):
                    piece = pl.ds(pl.multiple_of(c * CHUNK, CHUNK), CHUNK)
                    acc[:, piece] += jnp.dot(
                        cols[q, u, :, deep_span(h)], w_buf[deep_span(h), piece],
                        preferred_element_type=jnp.float32,
                    )

            take(n_gy - 1, u, parts - 1)
            out_copy(q, u).start()
            last = deep_span(parts - 1)

            @pl.loop(0, width // SEND)
            def _(c):
                for part in range(0, SEND, CHUNK):
                    piece = pl.ds(pl.multiple_of(c * SEND + part, CHUNK), CHUNK)
                    value = acc[:, piece] + jnp.dot(
                        cols[q, u, :, last], w_buf[last, piece], preferred_element_type=jnp.float32
                    )
                    part_send[q, u, :, :, piece] = value.astype(jnp.bfloat16).reshape(
                        ratio, rows_in, CHUNK
                    )
                send_parts(q, u, pl.ds(pl.multiple_of(c * SEND, SEND), SEND))

    pltpu.make_async_copy(part_send.at[0, 0, 0], part_recv.at[me], part_own_sem).wait()

    @pl.loop(1, plane)
    def _(i):
        other, where = plane_peer(i)
        pltpu.make_async_remote_copy(
            src_ref=part_send.at[0, 0, 0], dst_ref=part_recv.at[other],
            send_sem=part_ssem.at[other], recv_sem=part_rsem.at[other],
            device_id=where, device_id_type=MESH,
        ).wait_recv()

    row_sum = jnp.zeros((rows_in, 1), jnp.float32)
    row_dot = jnp.zeros((rows_in, 1), jnp.float32)
    for start in range(0, width, CHUNK):
        span = slice(start, start + CHUNK)
        block = lax.fori_loop(
            0, plane,
            lambda i, acc: acc + part_recv[i, :, span].astype(jnp.float32),
            jnp.zeros((rows_in, CHUNK), jnp.float32),
            unroll=8,
        )
        grad_normed[:, span] = block
        hat = x_hat[:, span]
        sums[me, 0:1, span] = jnp.sum(block * hat, axis=0, keepdims=True)
        sums[me, 1:2, span] = jnp.sum(block, axis=0, keepdims=True)
        scaled = block * row(gain, span)
        row_sum = row_sum + jnp.sum(scaled, axis=1, keepdims=True)
        row_dot = row_dot + jnp.sum(scaled * hat, axis=1, keepdims=True)
    stat_b[p] = to_tile(pad, row_sum, row_dot, rows_in)
    for i in range(1, n_gy):
        tile_copy(stat_b, i, last_send, last_recv, p).start()

    def sums_copy(i, source):
        other, where = plane_peer(i)
        return pltpu.make_async_remote_copy(
            src_ref=sums.at[source], dst_ref=sums.at[source],
            send_sem=sums_send.at[other], recv_sem=sums_recv.at[source],
            device_id=where, device_id_type=MESH,
        )

    @pl.loop(1, plane)
    def _(i):
        sums_copy(i, me).start()

    for i in range(1, n_gy):
        tile_copy(stat_b, i, last_send, last_recv, line_peer(i)).wait_recv()
    both = stat_b[0]
    for q in range(1, n_gy):
        both = both + stat_b[q]
    grad_sum, grad_dot = to_columns(pad, both, rows_in)
    for start in range(0, width, CHUNK):
        span = slice(start, start + CHUNK)
        scaled = grad_normed[:, span] * row(gain, span)
        grad_inputs[:, span] = (
            inv_std * (scaled - grad_sum / model - x_hat[:, span] * (grad_dot / model))
        ).astype(jnp.bfloat16)

    @pl.loop(1, plane)
    def _(i):
        sums_copy(i, plane_peer(i)[0]).wait_recv()

    grad_sums[...] = lax.fori_loop(
        0, plane, lambda i, acc: acc + sums[i], jnp.zeros((2, width), jnp.float32), unroll=8
    )

    norm_own.wait()

    @pl.loop(1, plane)
    def _(i):
        other, where = plane_peer(i)
        norm_copy(i, me).wait_send()
        norm_copy(i, other).wait_recv()
        sums_copy(i, me).wait_send()
        pltpu.make_async_remote_copy(
            src_ref=part_send.at[0, 0, 0], dst_ref=part_recv.at[me],
            send_sem=part_ssem.at[other], recv_sem=part_rsem.at[me],
            device_id=where, device_id_type=MESH,
        ).wait_send()

    for i in range(1, n_gy):
        tile_copy(stat_a, i, stat_send, stat_recv, p).wait_send()
        tile_copy(stat_b, i, last_send, last_recv, p).wait_send()
    for i in range(1, n_gx):
        u = lax.rem(g + i, n_gx)
        pltpu.make_async_remote_copy(
            src_ref=stage.at[u], dst_ref=cols.at[p, g],
            send_sem=x_send.at[u], recv_sem=z_recv.at[0],
            device_id={"gx": u}, device_id_type=MESH,
        ).wait_send()

    def sent(q, u, step, sems):
        return pltpu.make_async_remote_copy(
            src_ref=cols.at[q, u], dst_ref=cols.at[q, u],
            send_sem=sems.at[slot(q, u)], recv_sem=z_recv.at[0],
            device_id={"gy": lax.rem(p + step + n_gy, n_gy)}, device_id_type=MESH,
        )

    @pl.loop(0, n_gy)
    def _(q):
        for u in range(n_gx):
            out_copy(q, u).wait()

            @pl.when(jnp.logical_and(q <= p, p + 1 < n_gy))
            def _():
                sent(q, u, 1, right_send).wait_send()

            @pl.when(jnp.logical_and(q >= p, p >= 1))
            def _():
                sent(q, u, -1, left_send).wait_send()


def weight_kernel(cols, normed, inputs_in, sums_in, inputs_out, gain_out, bias_out, out):
    @pl.when(pl.program_id(0) == 0)
    def _():
        inputs_out[...] = inputs_in[...]
        gain_out[...] = sums_in[0]
        bias_out[...] = sums_in[1]

    out[...] = lax.dot_general(
        cols[...], normed[...], (((0,), (0,)), ((), ())), preferred_element_type=jnp.float32
    )


def on_device(shape, inputs, norm_gain, norm_bias, pre_act, grad_act, up_weight):
    n_gx, n_gy, n_gz = shape["gx"], shape["gy"], shape["gz"]
    plane = n_gx * n_gz
    rows_in, width = inputs.shape
    rows = pre_act.shape[0]
    depth = up_weight.shape[1]
    parts = next(n for n in (4, 3, 2, 1) if depth % (n * LANES) == 0)
    whole, vmem = pl.BlockSpec(memory_space=pl.ANY), pl.BlockSpec(memory_space=pltpu.VMEM)
    dma = pltpu.SemaphoreType.DMA
    bf16, f32 = jnp.bfloat16, jnp.float32
    ratio = rows // rows_in
    slots = n_gx * n_gy
    grad_cols, normed_all, grad_inputs, grad_sums = pl.pallas_call(
        functools.partial(kernel, (n_gx, n_gy, n_gz, rows, rows_in, width, depth, parts)),
        out_shape=(
            jax.ShapeDtypeStruct((n_gx, n_gy, rows, depth), bf16),
            jax.ShapeDtypeStruct((plane, rows_in, width), bf16),
            jax.ShapeDtypeStruct((rows_in, width), bf16),
            jax.ShapeDtypeStruct((2, width), f32),
        ),
        in_specs=[vmem, vmem, vmem, whole, whole, whole],
        out_specs=(whole, whole, vmem, vmem),
        scratch_shapes=[
            pltpu.VMEM((n_gx, rows, depth), bf16),
            pltpu.VMEM((n_gx, rows, depth), bf16),
            pltpu.VMEM((n_gx, rows, depth), bf16),
            pltpu.VMEM((depth, width), bf16),
            pltpu.VMEM((n_gy, n_gx, rows, depth), bf16),
            pltpu.VMEM((rows, width), f32),
            pltpu.VMEM((n_gy, n_gx, ratio, rows_in, width), bf16),
            pltpu.VMEM((plane, rows_in, width), bf16),
            pltpu.VMEM((rows_in, width), f32),
            pltpu.VMEM((rows_in, width), f32),
            pltpu.VMEM((rows_in, width), bf16),
            pltpu.VMEM((plane, 2, width), f32),
            pltpu.VMEM((LANES, LANES), f32),
            pltpu.VMEM((n_gy, SUB, LANES), f32),
            pltpu.VMEM((n_gy, SUB, LANES), f32),
            dma((n_gx * parts,)), dma((n_gx * parts,)), dma, dma((slots,)), dma((slots * parts,)), dma((slots,)), dma((slots,)), dma((n_gx,)),
            dma((n_gy,)), dma((n_gy,)), dma((plane,)), dma((plane,)), dma,
            dma((plane,)), dma((plane,)), dma,
            dma((plane,)), dma((plane,)), dma((n_gy,)), dma((n_gy,)),
        ],
        compiler_params=pltpu.CompilerParams(
            collective_id=0, has_side_effects=True, vmem_limit_bytes=60 * 1024 * 1024
        ),
    )(inputs, norm_gain, norm_bias, pre_act, grad_act, up_weight[0])
    tokens = slots * rows
    tile = next(n for n in (512, 384, 256, LANES) if depth % n == 0)
    fixed = lambda *shape: pl.BlockSpec(shape, lambda i: (0,) * len(shape))
    return pl.pallas_call(
        weight_kernel,
        grid=(depth // tile,),
        out_shape=(
            jax.ShapeDtypeStruct((rows_in, width), bf16),
            jax.ShapeDtypeStruct((width,), f32),
            jax.ShapeDtypeStruct((width,), f32),
            jax.ShapeDtypeStruct((1, depth, width), f32),
        ),
        in_specs=[
            pl.BlockSpec((tokens, tile), lambda i: (0, i)),
            fixed(tokens, width), fixed(rows_in, width), fixed(2, width),
        ],
        out_specs=(
            fixed(rows_in, width), fixed(width), fixed(width),
            pl.BlockSpec((None, tile, width), lambda i: (0, i, 0)),
        ),
        compiler_params=pltpu.CompilerParams(
            dimension_semantics=("arbitrary",), vmem_limit_bytes=48 * 1024 * 1024
        ),
        cost_estimate=pl.CostEstimate(
            flops=2 * tokens * depth * width, transcendentals=0,
            bytes_accessed=2 * tokens * (depth + width) + 4 * depth * width,
        ),
    )(grad_cols.reshape(tokens, depth), normed_all.reshape(tokens, width), grad_inputs, grad_sums)


def solution(mesh):
    in_specs = (
        P(("gx", "gz"), "gy"),
        P("gy"),
        P("gy"),
        P(("gx", "gy"), "gz"),
        P(("gx", "gy"), "gz"),
        P("gz", "gx", "gy"),
    )
    out_specs = (P(("gx", "gz"), "gy"), P("gy"), P("gy"), P("gz", "gx", "gy"))
    return jax.shard_map(
        functools.partial(on_device, dict(mesh.shape)),
        mesh=mesh, in_specs=in_specs, out_specs=out_specs, check_vma=False,
    )
```

```python
import functools

import jax
import jax.numpy as jnp
from jax import lax
from jax.experimental import pallas as pl
from jax.experimental.pallas import tpu as pltpu
from jax.sharding import PartitionSpec as P

MESH = pl.DeviceIdType.MESH
LANES = 128
SUB = 8
CHUNK = 256
SEND = 512

epsilon = 1e-05
root_half = 0.7071067811865476
gauss_norm = 0.3989422804014327


def to_tile(pad, first, second, rows):
    lane = lax.broadcasted_iota(jnp.int32, (rows, LANES), 1)
    pad[...] = jnp.zeros_like(pad)
    pad[:rows, :] = jnp.where(lane == 0, first, jnp.where(lane == 1, second, 0.0))
    return pad[...].T[:SUB, :]


def to_columns(pad, tile, rows):
    pad[...] = jnp.zeros_like(pad)
    pad[:SUB, :] = tile
    flipped = pad[...].T
    return flipped[:rows, 0:1], flipped[:rows, 1:2]


def kernel(
    sizes,
    inputs, gain, bias, pre_act, grad_act, weight,
    cols_out, normed_out, grad_inputs, grad_sums,
    pre_buf, act_buf, stage, w_buf, cols, acc, part_send, part_recv, x_hat, grad_normed, normed_own, sums, pad, stat_a, stat_b,
    pre_sem, act_sem, w_sem, out_sem, z_recv, right_send, left_send, x_send,
    stat_send, stat_recv, norm_send, norm_recv, norm_own_sem, part_ssem, part_rsem, part_own_sem,
    sums_send, sums_recv, last_send, last_recv,
):
    n_gx, n_gy, n_gz, rows, rows_in, width, depth, parts = sizes
    deep = depth // parts
    ratio = rows // rows_in
    plane = n_gx * n_gz
    g, p, t = lax.axis_index("gx"), lax.axis_index("gy"), lax.axis_index("gz")
    me = g * n_gz + t
    model = width * n_gy

    def line_peer(i):
        return lax.rem(p + i, n_gy)

    def plane_peer(i):
        other = lax.rem(me + i, plane)
        return other, {"gx": other // n_gz, "gz": lax.rem(other, n_gz)}

    def slot(q, u):
        return q * n_gx + u

    def row(ref, span):
        return ref[span].reshape(1, -1)

    barrier = pltpu.get_barrier_semaphore()
    for i in range(1, n_gy):
        pl.semaphore_signal(barrier, inc=1, device_id={"gy": line_peer(i)}, device_id_type=MESH)

    @pl.loop(1, plane)
    def _(i):
        pl.semaphore_signal(barrier, inc=1, device_id=plane_peer(i)[1], device_id_type=MESH)

    def deep_span(h, base=0):
        return pl.ds(pl.multiple_of(base + h * deep, LANES), deep)

    def load(u, h):
        source = deep_span(h, u * depth)
        return (
            pltpu.make_async_copy(
                pre_act.at[:, source], pre_buf.at[u, :, deep_span(h)], pre_sem.at[u * parts + h]
            ),
            pltpu.make_async_copy(
                grad_act.at[:, source], act_buf.at[u, :, deep_span(h)], act_sem.at[u * parts + h]
            ),
        )

    order = [lax.rem(g + i, n_gx) for i in list(range(1, n_gx)) + [0]]
    for h in range(parts):
        for u in order:
            for copy in load(u, h):
                copy.start()
    w_copy = pltpu.make_async_copy(weight, w_buf, w_sem)
    w_copy.start()

    step = next(n for n in (384, 256, LANES) if deep % n == 0)

    def gelu_grad(u, h, out):
        for copy in load(u, h):
            copy.wait()

        @pl.loop(0, deep // step)
        def _(c):
            span = pl.ds(pl.multiple_of(h * deep + c * step, LANES), step)
            pre = pre_buf[u, :, span].astype(jnp.float32)
            slopes = (
                0.5 * (1.0 + lax.erf(pre * root_half))
                + pre * jnp.exp(-0.5 * pre * pre) * gauss_norm
            )
            out[:, span] = (act_buf[u, :, span].astype(jnp.float32) * slopes).astype(jnp.bfloat16)

    def tile_copy(buf, i, ssem, rsem, source):
        return pltpu.make_async_remote_copy(
            src_ref=buf.at[source], dst_ref=buf.at[source],
            send_sem=ssem.at[line_peer(i)], recv_sem=rsem.at[source],
            device_id={"gy": line_peer(i)}, device_id_type=MESH,
        )

    def x_copy(i, source, h):
        u = lax.rem(g + i, n_gx)
        return pltpu.make_async_remote_copy(
            src_ref=stage.at[u, :, deep_span(h)],
            dst_ref=cols.at[p, source, :, deep_span(h)],
            send_sem=x_send.at[u], recv_sem=z_recv.at[slot(p, source) * parts + h],
            device_id={"gx": u}, device_id_type=MESH,
        )

    def z_copy(q, u, h, step, sems):
        return pltpu.make_async_remote_copy(
            src_ref=cols.at[q, u, :, deep_span(h)], dst_ref=cols.at[q, u, :, deep_span(h)],
            send_sem=sems.at[slot(q, u)], recv_sem=z_recv.at[slot(q, u) * parts + h],
            device_id={"gy": lax.rem(p + step + n_gy, n_gy)}, device_id_type=MESH,
        )

    def out_copy(q, u):
        return pltpu.make_async_copy(cols.at[q, u], cols_out.at[u, q], out_sem.at[slot(q, u)])

    def pass_right(q, u, h):
        @pl.when(p + 1 < n_gy)
        def _():
            z_copy(q, u, h, 1, right_send).start()

    def pass_left(q, u, h):
        @pl.when(p >= 1)
        def _():
            z_copy(q, u, h, -1, left_send).start()

    for h in range(parts):
        for i in range(1, n_gx):
            u = lax.rem(g + i, n_gx)
            gelu_grad(u, h, stage.at[u])
            if h == 0 and i == 1:
                pl.semaphore_wait(barrier, n_gy - 1 + plane - 1)
            x_copy(i, g, h).start()
        gelu_grad(g, h, cols.at[p, g])
        pass_right(p, g, h)
        pass_left(p, g, h)
    out_copy(p, g).start()

    widened = inputs[...].astype(jnp.float32)
    mean_here = jnp.sum(widened, axis=1, keepdims=True) / width
    centred = widened - mean_here
    square_here = jnp.sum(centred * centred, axis=1, keepdims=True)
    stat_a[p] = to_tile(pad, mean_here, square_here, rows_in)
    for i in range(1, n_gy):
        tile_copy(stat_a, i, stat_send, stat_recv, p).start()

    for i in range(1, n_gx):
        u = lax.rem(g + i, n_gx)

        @pl.loop(0, parts)
        def _(h):
            x_copy(i, u, h).wait_recv()
            pass_right(p, u, h)
            pass_left(p, u, h)

        out_copy(p, u).start()
    for i in range(1, n_gy):
        tile_copy(stat_a, i, stat_send, stat_recv, line_peer(i)).wait_recv()
    columns = [to_columns(pad, stat_a[q], rows_in) for q in range(n_gy)]
    mean = sum(c[0] for c in columns) / n_gy
    total = sum(c[1] + width * (c[0] - mean) * (c[0] - mean) for c in columns)
    inv_std = lax.rsqrt(total / model + epsilon)
    x_hat[...] = (inputs[...].astype(jnp.float32) - mean) * inv_std
    normed_own[...] = (x_hat[...] * row(gain, slice(None)) + row(bias, slice(None))).astype(jnp.bfloat16)

    def norm_copy(i, source):
        other, where = plane_peer(i)
        return pltpu.make_async_remote_copy(
            src_ref=normed_own, dst_ref=normed_out.at[source],
            send_sem=norm_send.at[other], recv_sem=norm_recv.at[source],
            device_id=where, device_id_type=MESH,
        )

    @pl.loop(1, plane)
    def _(i):
        norm_copy(i, me).start()

    norm_own = pltpu.make_async_copy(normed_own, normed_out.at[me], norm_own_sem)
    norm_own.start()

    w_copy.wait()

    def part_copy(q, u, j, source, span):
        owner = q * ratio + j
        return pltpu.make_async_remote_copy(
            src_ref=part_send.at[q, u, j, :, span], dst_ref=part_recv.at[source, :, span],
            send_sem=part_ssem.at[u * n_gz + owner], recv_sem=part_rsem.at[source],
            device_id={"gx": u, "gz": owner}, device_id_type=MESH,
        )

    def send_parts(q, u, span):
        for j in range(ratio):
            mine = jnp.logical_and(u == g, q * ratio + j == t)

            @pl.when(mine)
            def _():
                pltpu.make_async_copy(
                    part_send.at[q, u, j, :, span], part_recv.at[me, :, span], part_own_sem
                ).start()

            @pl.when(jnp.logical_not(mine))
            def _():
                part_copy(q, u, j, me, span).start()

    def multiply(q):
        @pl.loop(0, width // SEND)
        def _(c):
            for part in range(0, SEND, CHUNK):
                piece = pl.ds(pl.multiple_of(c * SEND + part, CHUNK), CHUNK)
                block = cols[q].reshape(n_gx * rows, depth)
                value = jnp.dot(block, w_buf[:, piece], preferred_element_type=jnp.float32)
                part_send[q, :, :, :, piece] = value.astype(jnp.bfloat16).reshape(
                    n_gx, ratio, rows_in, CHUNK
                )
            for u in range(n_gx):
                send_parts(q, u, pl.ds(pl.multiple_of(c * SEND, SEND), SEND))

    multiply(p)

    def take(s, u, h):
        @pl.when(p - s >= 0)
        def _():
            z_copy(p - s, u, h, 1, right_send).wait_recv()
            pass_right(p - s, u, h)

        @pl.when(p + s < n_gy)
        def _():
            z_copy(p + s, u, h, -1, left_send).wait_recv()
            pass_left(p + s, u, h)

    @pl.loop(1, n_gy - 1)
    def _(s):
        @pl.loop(0, n_gx * parts)
        def _(k):
            take(s, lax.rem(g + k // parts, n_gx), lax.rem(k, parts))

        @pl.loop(0, 2)
        def _(side):
            q = p + (2 * side - 1) * s

            @pl.when(jnp.logical_and(q >= 0, q < n_gy))
            def _():
                for u in range(n_gx):
                    out_copy(q, u).start()
                multiply(q)

    @pl.when(jnp.logical_or(p == 0, p == n_gy - 1))
    def _():
        q = n_gy - 1 - p

        @pl.loop(0, n_gx)
        def _(k):
            u = lax.rem(g + k, n_gx)
            acc[...] = jnp.zeros_like(acc)

            @pl.loop(0, parts - 1)
            def _(h):
                take(n_gy - 1, u, h)

                @pl.loop(0, width // CHUNK)
                def _(c):
                    piece = pl.ds(pl.multiple_of(c * CHUNK, CHUNK), CHUNK)
                    acc[:, piece] += jnp.dot(
                        cols[q, u, :, deep_span(h)], w_buf[deep_span(h), piece],
                        preferred_element_type=jnp.float32,
                    )

            take(n_gy - 1, u, parts - 1)
            out_copy(q, u).start()
            last = deep_span(parts - 1)

            @pl.loop(0, width // SEND)
            def _(c):
                for part in range(0, SEND, CHUNK):
                    piece = pl.ds(pl.multiple_of(c * SEND + part, CHUNK), CHUNK)
                    value = acc[:, piece] + jnp.dot(
                        cols[q, u, :, last], w_buf[last, piece], preferred_element_type=jnp.float32
                    )
                    part_send[q, u, :, :, piece] = value.astype(jnp.bfloat16).reshape(
                        ratio, rows_in, CHUNK
                    )
                send_parts(q, u, pl.ds(pl.multiple_of(c * SEND, SEND), SEND))

    pltpu.make_async_copy(part_send.at[0, 0, 0], part_recv.at[me], part_own_sem).wait()

    @pl.loop(1, plane)
    def _(i):
        other, where = plane_peer(i)
        pltpu.make_async_remote_copy(
            src_ref=part_send.at[0, 0, 0], dst_ref=part_recv.at[other],
            send_sem=part_ssem.at[other], recv_sem=part_rsem.at[other],
            device_id=where, device_id_type=MESH,
        ).wait_recv()

    row_sum = jnp.zeros((rows_in, 1), jnp.float32)
    row_dot = jnp.zeros((rows_in, 1), jnp.float32)
    for start in range(0, width, CHUNK):
        span = slice(start, start + CHUNK)
        block = lax.fori_loop(
            0, plane,
            lambda i, acc: acc + part_recv[i, :, span].astype(jnp.float32),
            jnp.zeros((rows_in, CHUNK), jnp.float32),
            unroll=8,
        )
        grad_normed[:, span] = block
        hat = x_hat[:, span]
        sums[me, 0:1, span] = jnp.sum(block * hat, axis=0, keepdims=True)
        sums[me, 1:2, span] = jnp.sum(block, axis=0, keepdims=True)
        scaled = block * row(gain, span)
        row_sum = row_sum + jnp.sum(scaled, axis=1, keepdims=True)
        row_dot = row_dot + jnp.sum(scaled * hat, axis=1, keepdims=True)
    stat_b[p] = to_tile(pad, row_sum, row_dot, rows_in)
    for i in range(1, n_gy):
        tile_copy(stat_b, i, last_send, last_recv, p).start()

    def sums_copy(i, source):
        other, where = plane_peer(i)
        return pltpu.make_async_remote_copy(
            src_ref=sums.at[source], dst_ref=sums.at[source],
            send_sem=sums_send.at[other], recv_sem=sums_recv.at[source],
            device_id=where, device_id_type=MESH,
        )

    @pl.loop(1, plane)
    def _(i):
        sums_copy(i, me).start()

    for i in range(1, n_gy):
        tile_copy(stat_b, i, last_send, last_recv, line_peer(i)).wait_recv()
    both = stat_b[0]
    for q in range(1, n_gy):
        both = both + stat_b[q]
    grad_sum, grad_dot = to_columns(pad, both, rows_in)
    for start in range(0, width, CHUNK):
        span = slice(start, start + CHUNK)
        scaled = grad_normed[:, span] * row(gain, span)
        grad_inputs[:, span] = (
            inv_std * (scaled - grad_sum / model - x_hat[:, span] * (grad_dot / model))
        ).astype(jnp.bfloat16)

    @pl.loop(1, plane)
    def _(i):
        sums_copy(i, plane_peer(i)[0]).wait_recv()

    grad_sums[...] = lax.fori_loop(
        0, plane, lambda i, acc: acc + sums[i], jnp.zeros((2, width), jnp.float32), unroll=8
    )

    norm_own.wait()

    @pl.loop(1, plane)
    def _(i):
        other, where = plane_peer(i)
        norm_copy(i, me).wait_send()
        norm_copy(i, other).wait_recv()
        sums_copy(i, me).wait_send()
        pltpu.make_async_remote_copy(
            src_ref=part_send.at[0, 0, 0], dst_ref=part_recv.at[me],
            send_sem=part_ssem.at[other], recv_sem=part_rsem.at[me],
            device_id=where, device_id_type=MESH,
        ).wait_send()

    for i in range(1, n_gy):
        tile_copy(stat_a, i, stat_send, stat_recv, p).wait_send()
        tile_copy(stat_b, i, last_send, last_recv, p).wait_send()
    for i in range(1, n_gx):
        u = lax.rem(g + i, n_gx)
        pltpu.make_async_remote_copy(
            src_ref=stage.at[u], dst_ref=cols.at[p, g],
            send_sem=x_send.at[u], recv_sem=z_recv.at[0],
            device_id={"gx": u}, device_id_type=MESH,
        ).wait_send()

    def sent(q, u, step, sems):
        return pltpu.make_async_remote_copy(
            src_ref=cols.at[q, u], dst_ref=cols.at[q, u],
            send_sem=sems.at[slot(q, u)], recv_sem=z_recv.at[0],
            device_id={"gy": lax.rem(p + step + n_gy, n_gy)}, device_id_type=MESH,
        )

    @pl.loop(0, n_gy)
    def _(q):
        for u in range(n_gx):
            out_copy(q, u).wait()

            @pl.when(jnp.logical_and(q <= p, p + 1 < n_gy))
            def _():
                sent(q, u, 1, right_send).wait_send()

            @pl.when(jnp.logical_and(q >= p, p >= 1))
            def _():
                sent(q, u, -1, left_send).wait_send()


def weight_kernel(cols, normed, inputs_in, sums_in, inputs_out, gain_out, bias_out, out):
    @pl.when(pl.program_id(0) == 0)
    def _():
        inputs_out[...] = inputs_in[...]
        gain_out[...] = sums_in[0]
        bias_out[...] = sums_in[1]

    out[...] = lax.dot_general(
        cols[...], normed[...], (((0,), (0,)), ((), ())), preferred_element_type=jnp.float32
    )


def on_device(shape, inputs, norm_gain, norm_bias, pre_act, grad_act, up_weight):
    n_gx, n_gy, n_gz = shape["gx"], shape["gy"], shape["gz"]
    plane = n_gx * n_gz
    rows_in, width = inputs.shape
    rows = pre_act.shape[0]
    depth = up_weight.shape[1]
    parts = next(n for n in (4, 3, 2, 1) if depth % (n * LANES) == 0)
    whole, vmem = pl.BlockSpec(memory_space=pl.ANY), pl.BlockSpec(memory_space=pltpu.VMEM)
    dma = pltpu.SemaphoreType.DMA
    bf16, f32 = jnp.bfloat16, jnp.float32
    ratio = rows // rows_in
    slots = n_gx * n_gy
    grad_cols, normed_all, grad_inputs, grad_sums = pl.pallas_call(
        functools.partial(kernel, (n_gx, n_gy, n_gz, rows, rows_in, width, depth, parts)),
        out_shape=(
            jax.ShapeDtypeStruct((n_gx, n_gy, rows, depth), bf16),
            jax.ShapeDtypeStruct((plane, rows_in, width), bf16),
            jax.ShapeDtypeStruct((rows_in, width), bf16),
            jax.ShapeDtypeStruct((2, width), f32),
        ),
        in_specs=[vmem, vmem, vmem, whole, whole, whole],
        out_specs=(whole, whole, vmem, vmem),
        scratch_shapes=[
            pltpu.VMEM((n_gx, rows, depth), bf16),
            pltpu.VMEM((n_gx, rows, depth), bf16),
            pltpu.VMEM((n_gx, rows, depth), bf16),
            pltpu.VMEM((depth, width), bf16),
            pltpu.VMEM((n_gy, n_gx, rows, depth), bf16),
            pltpu.VMEM((rows, width), f32),
            pltpu.VMEM((n_gy, n_gx, ratio, rows_in, width), bf16),
            pltpu.VMEM((plane, rows_in, width), bf16),
            pltpu.VMEM((rows_in, width), f32),
            pltpu.VMEM((rows_in, width), f32),
            pltpu.VMEM((rows_in, width), bf16),
            pltpu.VMEM((plane, 2, width), f32),
            pltpu.VMEM((LANES, LANES), f32),
            pltpu.VMEM((n_gy, SUB, LANES), f32),
            pltpu.VMEM((n_gy, SUB, LANES), f32),
            dma((n_gx * parts,)), dma((n_gx * parts,)), dma, dma((slots,)), dma((slots * parts,)), dma((slots,)), dma((slots,)), dma((n_gx,)),
            dma((n_gy,)), dma((n_gy,)), dma((plane,)), dma((plane,)), dma,
            dma((plane,)), dma((plane,)), dma,
            dma((plane,)), dma((plane,)), dma((n_gy,)), dma((n_gy,)),
        ],
        compiler_params=pltpu.CompilerParams(
            collective_id=0, has_side_effects=True, vmem_limit_bytes=60 * 1024 * 1024
        ),
    )(inputs, norm_gain, norm_bias, pre_act, grad_act, up_weight[0])
    tokens = slots * rows
    tile = next(n for n in (512, 384, 256, LANES) if depth % n == 0)
    fixed = lambda *shape: pl.BlockSpec(shape, lambda i: (0,) * len(shape))
    return pl.pallas_call(
        weight_kernel,
        grid=(depth // tile,),
        out_shape=(
            jax.ShapeDtypeStruct((rows_in, width), bf16),
            jax.ShapeDtypeStruct((width,), f32),
            jax.ShapeDtypeStruct((width,), f32),
            jax.ShapeDtypeStruct((1, depth, width), f32),
        ),
        in_specs=[
            pl.BlockSpec((tokens, tile), lambda i: (0, i)),
            fixed(tokens, width), fixed(rows_in, width), fixed(2, width),
        ],
        out_specs=(
            fixed(rows_in, width), fixed(width), fixed(width),
            pl.BlockSpec((None, tile, width), lambda i: (0, i, 0)),
        ),
        compiler_params=pltpu.CompilerParams(
            dimension_semantics=("arbitrary",), vmem_limit_bytes=67_043_328
        ),
        cost_estimate=pl.CostEstimate(
            flops=2 * tokens * depth * width, transcendentals=0,
            bytes_accessed=2 * tokens * (depth + width) + 4 * depth * width,
        ),
    )(grad_cols.reshape(tokens, depth), normed_all.reshape(tokens, width), grad_inputs, grad_sums)


def solution(mesh):
    in_specs = (
        P(("gx", "gz"), "gy"),
        P("gy"),
        P("gy"),
        P(("gx", "gy"), "gz"),
        P(("gx", "gy"), "gz"),
        P("gz", "gx", "gy"),
    )
    out_specs = (P(("gx", "gz"), "gy"), P("gy"), P("gy"), P("gz", "gx", "gy"))
    return jax.shard_map(
        functools.partial(on_device, dict(mesh.shape)),
        mesh=mesh, in_specs=in_specs, out_specs=out_specs, check_vma=False,
    )
```
